256 devices in a mesh: sample: 16 (over z, core), expert: 16 (over y, x).
Axes of the slice: x: 4, y: 4, z: 8, core: 2. Of those that a mesh axis runs over, the one named last changes fastest.
Arguments:
- queries: bfloat16 [128, 16, 8192], P('expert', 'sample'), may hold values from -8 to 8
- prompt_kv: bfloat16 [128, 1024, 1024], P('expert', 'sample'), may hold values from -8 to 8
- gen_kv: bfloat16 [128, 16, 32, 1024], P('expert', 'sample'), may hold values from -4 to 4
- gen_lengths: int32 [128, 16], P('expert', 'sample'), may hold values from 1 to 32, 256 in all within a row
- out_proj: bfloat16 [8192, 4096], P(None, 'sample'), may hold values from -1 to 1
- residual: bfloat16 [128, 16, 4096], P('expert', None, 'sample'), may hold values from -160 to 160
- norm_gain: float32 [4096], P('sample'), may hold values from 0.1 to 1.9
- w_gate_up: bfloat16 [48, 4096, 3072], P('expert', 'sample'), may hold values from -0.09375 to 0.09375
- w_down: bfloat16 [48, 1536, 4096], P('expert', None, 'sample'), may hold values from -0.15625 to 0.15625
- routes: int32 [128, 16, 8], P('expert'), may hold values from 0 to 47, all different within a row; in each aligned block of 128 rows (0 to 127, 128 to 255, ..., all dimensions but the last counted through in order) at most 26 rows name the same one
- route_probs: float32 [128, 16, 8], P('expert'), may hold values from 0.1 to 1
Outputs:
- mixed: bfloat16 [128, 16, 4096], P('expert', None, 'sample')
- expert_out: bfloat16 [128, 16, 4096], P('expert', None, 'sample')
The draws below stay inside these ranges and needn't reach their ends.
Inputs may be any that keep to these rules, and one draw needn't show every extreme that they name: `gen_lengths`: in each prompt, at least one sample has 32 generated tokens. `routes`: each row names 8 different experts. Among the 128 rows of the prompts of one index of expert, no expert is named by more than 26 rows, a bound that some block reaches.
All inputs are finite; a program needn't handle non-finite values. No bound on the sum of `gen_lengths` on one device may be relied on, other than what follows from the above.
Results may differ from the reference program's by a relative error of at most 0.028.
Values may be sent and summed in bfloat16 or wider, within the bound.
A program may use at most 128 MiB of HBM per device.

```python
import math
import jax
import jax.numpy as jnp
import numpy as np
from jax import lax

D = 4096
FF = 1536
QHEADS = 64
KVHEADS = 4
HDIM = 128
TOPK = 8
PROMPTS_DEV = 8
GEN = 32
SAMPLES = 16
PROMPTS = 128
PLEN = 1024
WIN_EXPERTS = 48
CAP = 26
N_SAMPLE = 16
N_EXPERT = 16


def draw_queries(key, part):
    shape = (PROMPTS, SAMPLES, QHEADS * HDIM)
    values = jnp.clip(jax.random.normal(jax.random.fold_in(key, 1), shape, jnp.float32), -4.0, 4.0)
    return values.astype(jnp.bfloat16)


def draw_prompt_kv(key, part):
    width = 2 * KVHEADS * HDIM
    shape = (PROMPTS, PLEN, width)
    values = jnp.clip(jax.random.normal(jax.random.fold_in(key, 3), shape, jnp.float32), -4.0, 4.0)
    return values.astype(jnp.bfloat16)


def draw_residual(key, part):
    shape = (PROMPTS, SAMPLES, D)
    feature = jnp.arange(D, dtype=jnp.float32) / D
    values = jnp.clip(jax.random.normal(jax.random.fold_in(key, 5), shape, jnp.float32), -4.0, 4.0)
    row_scale = jnp.exp(jax.random.uniform(jax.random.fold_in(key, 8), (PROMPTS, SAMPLES, 1), jnp.float32, math.log(0.5), math.log(5.0)))
    rising = 1.0 + 2.0 * feature
    return (values * row_scale * rising[None, None, :]).astype(jnp.bfloat16)


def shard_levels(own_key, extent, cuts, least, largest):
    def one(dim, shards_of):
        steps = jax.random.uniform(jax.random.fold_in(jax.random.fold_in(own_key, 6), dim), (shards_of,), jnp.float32, least / len(cuts), largest / len(cuts))
        return jnp.repeat(jnp.exp(steps), extent[dim] // shards_of).reshape((-1,) + (1,) * (len(extent) - dim - 1))

    level = one(*cuts[0])
    for cut in cuts[1:]:
        level = level * one(*cut)
    return level


def length_profile(number_of, total, reach, slope):
    loads = [(1 << 20) // math.isqrt(standing ** slope) + 1 for standing in range(2, number_of + 1)]
    rest, holding = total - reach - (number_of - 1), [1] * (number_of - 1)
    while rest > 0:
        free = [i for i in range(number_of - 1) if holding[i] < reach]
        whole, remaining = sum([loads[i] for i in free]), rest
        for i in free:
            extra = min(reach - holding[i], max(1, remaining * loads[i] // whole), rest)
            holding[i] = holding[i] + extra
            rest = rest - extra
    return np.array([reach] + holding)


def ragged(stream_key, count, total, reach, skew):
    if count == 2:
        one = jax.random.randint(stream_key, (), max(1, total - reach), min(reach, total - 1) + 1)
        return jnp.stack([one, total - one])
    sizes = jnp.asarray(length_profile(count, total, reach, skew), jnp.int32)
    couples = (count - 1) // 2
    donor, sink = sizes[1:1 + 2 * couples:2], sizes[2:2 + 2 * couples:2]
    slack = jnp.minimum(donor - 1, reach - sink)
    shifted = jax.random.randint(jax.random.fold_in(stream_key, 1), (couples,), 0, 1 << 20) % (slack + 1)
    sizes = sizes.at[1:1 + 2 * couples:2].set(donor - shifted).at[2:2 + 2 * couples:2].set(sink + shifted)
    return sizes[jax.random.permutation(jax.random.fold_in(stream_key, 2), count)]


def routed_block(rng, own, number, rows, count, top, most, lean):
    order = jax.random.permutation(rng, count)
    packed, ordinary = portions_of(count, rows * top, most, lean, True), portions_of(count, rows * top, most, lean, False)
    places = jnp.arange(count)

    def named(sizes, offset_by):
        used = int((sizes > 0).sum())
        fixed = max(1, used // 4)
        moved = fixed + (places - fixed + offset_by * (used - fixed)) % max(1, count - fixed)
        return jnp.zeros((count,), jnp.int32).at[order[jnp.where(places < fixed, places, moved)]].set(jnp.asarray(sizes, jnp.int32))

    sizes = jnp.where(number % 4 == 0, named(packed, number // 4), named(ordinary, number - number // 4 - 1))
    mixed = jax.random.permutation(jax.random.fold_in(own, 3), count)
    source_of, sink = mixed[0:count // 2 * 2:2], mixed[1:count // 2 * 2:2]
    margin = jnp.minimum(sizes[source_of] - 1, most - sizes[sink]) // 2
    margin = jnp.where((source_of == order[0]) | (sink == order[0]) | (sizes[sink] == 0), 0, jnp.maximum(margin, 0))
    moved = jax.random.randint(jax.random.fold_in(own, 4), (count // 2,), 0, 1 << 20) % (margin + 1)
    sizes = sizes.at[source_of].add(-moved).at[sink].add(moved)
    labels = jnp.searchsorted(jnp.cumsum(sizes), jnp.arange(rows * top), side="right").astype(jnp.int32)
    table = labels.reshape(top, rows).T
    table = table[jax.random.permutation(jax.random.fold_in(own, 1), rows)]
    offset_by = jax.random.randint(jax.random.fold_in(own, 2), (rows, 1), 0, top)
    return jnp.take_along_axis(table, (jnp.arange(top)[None, :] + offset_by) % top, axis=1)


def portions_of(number_of, total, bound, slope, full):
    portions = [(1 << 20) // math.isqrt(rank ** slope) + 1 for rank in range(1, number_of + 1)]
    largest = bound if full else min(bound, max(-(-total // number_of), total * portions[0] // sum(portions)))
    least = 1 if total - largest >= number_of - 1 else 0
    given, spare = [largest] + [least] * (number_of - 1), total - largest - least * (number_of - 1)
    while spare > 0:
        movable = [i for i in range(1, number_of) if given[i] < largest] or [i for i in range(1, number_of) if given[i] < bound]
        whole, remaining = sum([portions[i] for i in movable]), spare
        for i in movable:
            more = min(bound - given[i], max(1, remaining * portions[i] // whole), spare)
            given[i] = given[i] + more
            spare = spare - more
    return np.array(given)


def centred(stream_key, shape, deviation, most, cuts=(), kind=jnp.bfloat16):
    drawn = jax.random.normal(stream_key, shape, jnp.float32) * deviation
    if len(cuts) > 0:
        drawn = shard_levels(stream_key, shape, cuts, -0.22, 0.18) * drawn
    return jnp.clip(drawn, min=-most, max=most).astype(kind)


def setup_inputs(seed: int = 0) -> dict:
    arg_keys = jax.random.split(jax.random.key(seed), 12)
    queries = draw_queries(jax.random.fold_in(arg_keys[11], 71), 0)
    prompt_kv = draw_prompt_kv(jax.random.fold_in(arg_keys[11], 71), 0)
    gen_kv = centred(arg_keys[2], (PROMPTS, SAMPLES, GEN, 2 * KVHEADS * HDIM), 1.0, 4.0, ((0, 16), (1, 16)))
    gen_lengths = jax.vmap(lambda own: ragged(own, SAMPLES, SAMPLES * GEN // 2, GEN, 2))(jax.random.split(arg_keys[3], PROMPTS)).reshape((PROMPTS, SAMPLES)).astype(jnp.int32)
    out_proj = centred(arg_keys[4], (QHEADS * HDIM, D), (max(QHEADS * HDIM // 256, 1)) ** -0.5, 1.0, ((1, 16),))
    residual = draw_residual(jax.random.fold_in(arg_keys[11], 71), 0)
    norm_gain = jnp.clip(1.0 + 0.18 * jax.random.normal(arg_keys[6], (D,), jnp.float32), 0.1, 1.9)
    w_gate_up = centred(arg_keys[7], (WIN_EXPERTS, D, 2 * FF), D ** -0.5, 0.09375, ((0, 16), (1, 16)))
    w_down = centred(arg_keys[8], (WIN_EXPERTS, FF, D), FF ** -0.5, 0.15625, ((0, 16), (2, 16)))
    routes_keys = jax.random.split(jax.random.fold_in(arg_keys[9], 1), PROMPTS * SAMPLES // (PROMPTS_DEV * SAMPLES))
    routes_turns = jax.random.permutation(jax.random.fold_in(arg_keys[9], 3), PROMPTS * SAMPLES // (PROMPTS_DEV * SAMPLES))
    routes = jax.vmap(lambda own, number: routed_block(jax.random.fold_in(arg_keys[9], 2), own, number, PROMPTS_DEV * SAMPLES, WIN_EXPERTS, TOPK, CAP, 2))(routes_keys, routes_turns).reshape((PROMPTS, SAMPLES, TOPK))
    route_probs = jnp.clip(jnp.exp(math.log(1.0) - 2.3025851 * jax.random.uniform(arg_keys[10], (PROMPTS, SAMPLES, TOPK), jnp.float32) ** shard_levels(arg_keys[10], (PROMPTS, SAMPLES, TOPK), ((0, 16),), -0.2, 0.2)), 0.1, 1.0)
    return {"queries": queries, "prompt_kv": prompt_kv, "gen_kv": gen_kv, "gen_lengths": gen_lengths, "out_proj": out_proj, "residual": residual, "norm_gain": norm_gain, "w_gate_up": w_gate_up, "w_down": w_down, "routes": routes, "route_probs": route_probs}


NEGATIVE = -1e+30
EPSILON = 1e-06

def attend_prompt(operands):
    query, prompt, cache, lengths = operands
    kv_width = KVHEADS * HDIM
    groups = QHEADS // KVHEADS
    scale = HDIM ** (-0.5)
    heads = query.astype(jnp.float32).reshape(SAMPLES, KVHEADS, groups, HDIM)
    prompt_keys = prompt[:, :kv_width].astype(jnp.float32).reshape(PLEN, KVHEADS, HDIM)
    prompt_values = prompt[:, kv_width:].astype(jnp.float32).reshape(PLEN, KVHEADS, HDIM)
    cache_keys = cache[:, :, :kv_width].astype(jnp.float32).reshape(SAMPLES, GEN, KVHEADS, HDIM)
    cache_values = cache[:, :, kv_width:].astype(jnp.float32).reshape(SAMPLES, GEN, KVHEADS, HDIM)
    prompt_scores = jnp.einsum('shgd,nhd->shgn', heads, prompt_keys, precision=lax.Precision.HIGHEST) * scale
    cache_scores = jnp.einsum('shgd,sthd->shgt', heads, cache_keys, precision=lax.Precision.HIGHEST) * scale
    valid = jnp.arange(GEN, dtype=jnp.int32)[None, :] < lengths[:, None]
    cache_scores = jnp.where(valid[:, None, None, :], cache_scores, NEGATIVE)
    highest = jnp.maximum(lax.optimization_barrier(jnp.max(prompt_scores, axis=-1)), lax.optimization_barrier(jnp.max(cache_scores, axis=-1)))
    prompt_weights = jnp.exp(prompt_scores - highest[..., None])
    cache_weights = jnp.exp(cache_scores - highest[..., None])
    weight_sum = lax.optimization_barrier(jnp.sum(prompt_weights, axis=-1)) + lax.optimization_barrier(jnp.sum(cache_weights, axis=-1))
    numerator = jnp.einsum('shgn,nhd->shgd', prompt_weights, prompt_values, precision=lax.Precision.HIGHEST)
    numerator = numerator + jnp.einsum('shgt,sthd->shgd', cache_weights, cache_values, precision=lax.Precision.HIGHEST)
    return (numerator / weight_sum[..., None]).reshape(SAMPLES, QHEADS * HDIM).astype(jnp.bfloat16)

def reference(queries, prompt_kv, gen_kv, gen_lengths, out_proj, residual, norm_gain, w_gate_up, w_down, routes, route_probs):
    attended = lax.map(attend_prompt, (queries, prompt_kv, gen_kv, gen_lengths))
    projected = jnp.dot(attended.reshape(-1, QHEADS * HDIM), out_proj, preferred_element_type=jnp.float32)
    projected = projected.reshape(PROMPTS, SAMPLES, D)
    mixed = projected.astype(jnp.bfloat16)
    stream = residual.astype(jnp.float32) + projected
    factor = lax.rsqrt(lax.optimization_barrier(jnp.sum(stream * stream, axis=-1)) / D + EPSILON)
    normed = (stream * factor[..., None] * norm_gain).astype(jnp.bfloat16).reshape(-1, D)
    expert_ids = routes.reshape(-1, TOPK)
    route_weight = route_probs.reshape(-1, TOPK)
    block_width = D // N_SAMPLE
    limit = N_EXPERT * CAP

    def one_expert(running, expert):
        chosen = expert_ids == expert
        weight = lax.optimization_barrier(jnp.sum(jnp.where(chosen, route_weight, 0.0), axis=1))
        flagged = jnp.any(chosen, axis=1).astype(jnp.int32)
        order = jnp.argsort(1 - flagged, stable=True)[:limit].astype(jnp.int32)
        picked = normed[order].astype(jnp.float32).reshape(limit, N_SAMPLE, block_width)
        blocks = w_gate_up[expert].astype(jnp.float32).reshape(N_SAMPLE, block_width, 2 * FF)
        partial_sums = jnp.einsum('nbd,bdf->nbf', picked, blocks, precision=lax.Precision.HIGHEST)
        rounded = lax.optimization_barrier(partial_sums.astype(jnp.bfloat16))
        gate_up = lax.optimization_barrier(jnp.sum(rounded.astype(jnp.float32), axis=1))
        activated = (jax.nn.silu(gate_up[:, :FF]) * gate_up[:, FF:]).astype(jnp.bfloat16)
        finished = jnp.dot(activated, w_down[expert], preferred_element_type=jnp.float32).astype(jnp.bfloat16)
        finished = lax.optimization_barrier(finished).astype(jnp.float32)
        return (running.at[order].add(finished * weight[order][:, None]), None)
    running = jnp.zeros((normed.shape[0], D), jnp.float32)
    running, unused = lax.scan(one_expert, running, jnp.arange(WIN_EXPERTS, dtype=jnp.int32))
    expert_out = running.astype(jnp.bfloat16).reshape(PROMPTS, SAMPLES, D)
    return (mixed, expert_out)
```

```python
import functools

import jax
import jax.numpy as jnp
from jax import lax
from jax.experimental import pallas as pl
from jax.experimental.pallas import tpu as pltpu
from jax.sharding import PartitionSpec as P

MESH = pl.DeviceIdType.MESH
HDIM = 128
GROUPS = 16
HEADS_HERE = 2
EXP_COL = 3
CAP = 26
TILE = 16
NEGATIVE = -1e30
EPSILON = 1e-06
F32 = jnp.float32
BF16 = jnp.bfloat16


def remote(src, dst, send, recv, device):
    return pltpu.make_async_remote_copy(
        src_ref=src, dst_ref=dst, send_sem=send, recv_sem=recv, device_id=device, device_id_type=MESH
    )


def greet(groups):
    barrier = pltpu.get_barrier_semaphore()
    total = 0
    for axis, size in groups:
        me = lax.axis_index(axis)

        def signal(o, carry, axis=axis, size=size, me=me):
            pl.semaphore_signal(
                barrier, inc=1, device_id={axis: lax.rem(me + o, size)}, device_id_type=MESH
            )
            return carry

        lax.fori_loop(1, size, signal, 0)
        total += size - 1
    pl.semaphore_wait(barrier, total)


def attend_kernel(
    n, q, kv, gkv, wo, res, gain, mixed, normed,
    rq, rk, rv, rgk, rgv, wov, obuf, att, sqs, sqr,
    lsem, ssem, rsem, ag_s, ag_r, sib_s, sib_r, own_sem, sq_ss, sq_rs,
):
    chips = n // 2
    half = chips // 2
    me = lax.axis_index("sample")
    z, c = me // 2, lax.rem(me, 2)
    wide = HEADS_HERE * HDIM
    values_at = 2 * wide

    def pieces(p, hp, slot):
        return (
            (q.at[p, hp], rq.at[slot]),
            (kv.at[p, :, pl.ds(hp * wide, wide)], rk.at[slot]),
            (kv.at[p, :, pl.ds(values_at + hp * wide, wide)], rv.at[slot]),
            (gkv.at[p, :, pl.ds(hp * wide, wide)], rgk.at[slot]),
            (gkv.at[p, :, pl.ds(values_at + hp * wide, wide)], rgv.at[slot]),
        )

    greet((("sample", n),))
    order = sorted(range(1, chips), key=lambda d: -min(d, chips - d))
    sent = []
    for dz in order:
        p = lax.rem(z + dz, chips)
        for hp in range(2):
            for k, (src, dst) in enumerate(pieces(p, hp, me)):
                copy = remote(src, dst, ssem.at[k, 2 * dz + hp], rsem.at[k, me], {"sample": 2 * p + hp})
                copy.start()
                sent.append(copy)
    other = 1 - c
    dyn = pl.multiple_of(other * wide, wide)
    mine = pl.multiple_of(c * wide, wide)

    def pieces_dyn(hp, off, slot):
        return (
            (q.at[z, hp], rq.at[slot]),
            (kv.at[z, :, pl.ds(off, wide)], rk.at[slot]),
            (kv.at[z, :, pl.ds(pl.multiple_of(values_at + off, wide), wide)], rv.at[slot]),
            (gkv.at[z, :, pl.ds(off, wide)], rgk.at[slot]),
            (gkv.at[z, :, pl.ds(pl.multiple_of(values_at + off, wide), wide)], rgv.at[slot]),
        )

    for k, (src, dst) in enumerate(pieces_dyn(other, dyn, me)):
        copy = remote(src, dst, ssem.at[k, 0], rsem.at[k, me], {"sample": 2 * z + other})
        copy.start()
        sent.append(copy)
    local = []
    for k, (src, dst) in enumerate(pieces_dyn(c, mine, me)):
        copy = pltpu.make_async_copy(src, dst, lsem.at[k])
        copy.start()
        local.append(copy)
    weights = pltpu.make_async_copy(wo, wov, lsem.at[5])
    weights.start()
    for copy in local:
        copy.wait()

    def arrive(o, carry):
        src = lax.rem(me + o, n)
        for k, (a, b) in enumerate(pieces(0, 0, src)):
            remote(a, b, ssem.at[k, 1], rsem.at[k, src], {"sample": src}).wait_recv()
        return carry

    lax.fori_loop(1, n, arrive, 0)

    tokens = rk.shape[0] * rk.shape[1]
    gen = rgk.shape[1]
    block = 4
    scale = HDIM ** (-0.5)
    contract = (((1,), (1,)), ((), ()))
    for h in range(HEADS_HERE):
        lanes = slice(h * HDIM, (h + 1) * HDIM)

        def attend(i, carry, h=h, lanes=lanes):
            own = pl.ds(i * block, block)
            query = rq[own, h * GROUPS:(h + 1) * GROUPS, :].reshape(block * GROUPS, HDIM)
            length = rq[own, 2 * GROUPS:3 * GROUPS, :].reshape(block * GROUPS, HDIM).astype(F32)[:, 0:1]
            keys = rk[:, :, lanes].reshape(tokens, HDIM)
            vals = rv[:, :, lanes].reshape(tokens, HDIM)
            gkeys = rgk[own, :, lanes].reshape(block * gen, HDIM)
            gvals = rgv[own, :, lanes].reshape(block * gen, HDIM)
            scores = lax.dot_general(query, keys, contract, preferred_element_type=F32) * scale
            gscores = lax.dot_general(query, gkeys, contract, preferred_element_type=F32) * scale
            row = lax.broadcasted_iota(jnp.int32, gscores.shape, 0) // GROUPS
            col = lax.broadcasted_iota(jnp.int32, gscores.shape, 1)
            place = (col - row * gen).astype(F32)
            valid = jnp.logical_and(place >= 0.0, place < length)
            gscores = jnp.where(valid, gscores, NEGATIVE)
            highest = jnp.maximum(
                jnp.max(scores, axis=1, keepdims=True), jnp.max(gscores, axis=1, keepdims=True)
            )
            weight = jnp.exp(scores - highest)
            gweight = jnp.exp(gscores - highest)
            total = jnp.sum(weight, axis=1, keepdims=True) + jnp.sum(gweight, axis=1, keepdims=True)
            out = jnp.dot(weight.astype(BF16), vals, preferred_element_type=F32)
            out = out + jnp.dot(gweight.astype(BF16), gvals, preferred_element_type=F32)
            rows = pl.ds(pl.multiple_of(i * block * GROUPS, block * GROUPS), block * GROUPS)
            obuf[h, rows, :] = (out / total).astype(BF16)
            return carry

        lax.fori_loop(0, n // block, attend, 0)

    count = n * GROUPS
    r = lax.broadcasted_iota(jnp.int32, (count, count), 0)
    k = lax.broadcasted_iota(jnp.int32, (count, count), 1)
    swap = (k == (lax.rem(r, n) * GROUPS + r // n)).astype(F32).astype(BF16)
    at = pl.ds(pl.multiple_of(z * n, n), n)
    for h in range(HEADS_HERE):
        swapped = jnp.dot(swap, obuf[h], preferred_element_type=F32).astype(BF16)
        for g in range(GROUPS):
            first = (h * GROUPS + g) * HDIM
            att[c, at, first:first + HDIM] = swapped[g * n:(g + 1) * n, :]

    width = HEADS_HERE * GROUPS * HDIM
    cut = width // 2
    right = {"sample": 2 * lax.rem(z + 1, chips) + c}
    left = {"sample": 2 * lax.rem(z + chips - 1, chips) + c}
    ways = (right, left)
    sibling = {"sample": 2 * z + other}

    def part(core, b, u):
        return att.at[core, pl.ds(pl.multiple_of(b * n, n), n), u * cut:(u + 1) * cut]

    def goes(t, d, u):
        return t < half - 1 or (t == half - 1 and u == d)

    def start(copy):
        copy.start()
        sent.append(copy)

    for u in range(2):
        for d in range(2):
            if goes(0, d, u):
                start(remote(part(c, z, u), part(c, z, u), ag_s.at[d, 0, u], ag_r.at[d, 0, u], ways[d]))
    whole = att.at[c, at, :]
    start(remote(whole, whole, own_sem.at[0], own_sem.at[1], sibling))
    for t in range(half):
        for u in range(2):
            for d in range(2):
                if not goes(t, d, u):
                    continue
                b = lax.rem(z + (chips - 1 - t if d == 0 else 1 + t), chips)
                got = part(c, b, u)
                remote(got, got, ag_s.at[d, t, u], ag_r.at[d, t, u], ways[d]).wait_recv()
                if goes(t + 1, d, u):
                    start(remote(got, got, ag_s.at[d, t + 1, u], ag_r.at[d, t + 1, u], ways[d]))
                start(remote(got, got, sib_s.at[d, t, u], sib_r.at[d, t, u], sibling))
    theirs = att.at[other, at, :]
    remote(theirs, theirs, own_sem.at[0], own_sem.at[1], sibling).wait_recv()
    for t in range(half):
        for u in range(2):
            for d in range(2):
                if goes(t, d, u):
                    b = lax.rem(z + (chips - 1 - t if d == 0 else 1 + t), chips)
                    got = part(other, b, u)
                    remote(got, got, sib_s.at[d, t, u], sib_r.at[d, t, u], sibling).wait_recv()
    weights.wait()
    rows_all = res.shape[0]
    features = res.shape[1]
    step = min(1024, width)
    projected = jnp.zeros((rows_all, features), F32)
    for core in range(2):

        def project(i, acc, core=core):
            depth = pl.ds(pl.multiple_of(i * step, step), step)
            return acc + jnp.dot(att[core, :, depth], wov[core, depth, :], preferred_element_type=F32)

        projected = lax.fori_loop(0, width // step, project, projected)
    mixed[...] = projected.astype(BF16)
    stream = res[...].astype(F32) + projected
    eye = lax.broadcasted_iota(jnp.int32, (rows_all, rows_all), 0) == lax.broadcasted_iota(
        jnp.int32, (rows_all, rows_all), 1
    )
    column = jnp.sum(stream * stream, axis=1, keepdims=True)
    across = jnp.sum(jnp.where(eye, column, 0.0), axis=0, keepdims=True)
    sqs[...] = jnp.broadcast_to(across, sqs.shape)
    for o in range(1, n):
        to = lax.rem(me + o, n)
        start(remote(sqs, sqr.at[o], sq_ss.at[o], sq_rs.at[o], {"sample": to}))
    squares = sqs[...]
    for o in range(1, n):
        remote(sqs, sqr.at[o], sq_ss.at[o], sq_rs.at[o], {"sample": lax.rem(me + n - o, n)}).wait_recv()
        squares = squares + sqr[o]
    factor = lax.rsqrt(squares / (features * n) + EPSILON)
    down = jnp.sum(jnp.where(eye, factor[0:1, :], 0.0), axis=1, keepdims=True)
    normed[...] = (stream * down * gain[...]).astype(BF16)
    for copy in sent:
        copy.wait_send()


def spans():
    out = []
    for j in range(EXP_COL):
        low = CAP * j // TILE * TILE
        high = -(-CAP * (j + 1) // TILE) * TILE
        out.append((low, high))
    return out


def expert_kernel(
    n, e, x, pick, chi, clo, wgu, wdn, out,
    xs, xr, xm0, xm1, xm2, wg, wd, pown, psib, rsib, rr, act, osend, oret,
    lsem, x_s, x_r, sib_s, sib_r, rs_s, rs_r, ag_s, ag_r, fw_s, fw_r, me_sem, o_s, o_r,
):
    chips = n // 2
    half = chips // 2
    each = e // chips
    me = lax.axis_index("sample")
    z, c = me // 2, lax.rem(me, 2)
    other = 1 - c
    col = lax.axis_index("expert")
    shift = each * (col // each)
    unit = xs.shape[1]
    quarter = pown.shape[3] // 2
    ff = 4 * quarter
    features = x.shape[1]
    right = {"sample": 2 * lax.rem(z + 1, chips) + c}
    left = {"sample": 2 * lax.rem(z + chips - 1, chips) + c}
    ways = (right, left)
    sibling = {"sample": 2 * z + other}
    xm = (xm0, xm1, xm2)

    w1 = pltpu.make_async_copy(wgu, wg, lsem.at[0])
    w1.start()
    w2 = pltpu.make_async_copy(wdn, wd, lsem.at[1])
    w2.start()
    greet((("sample", n), ("expert", e)))
    sent = []

    def start(copy):
        copy.start()
        sent.append(copy)

    chosen = jnp.dot(pick[...], x[...], preferred_element_type=F32).astype(BF16)
    xs[...] = chosen.reshape(e, unit, features)
    for o in range(1, e):
        to = lax.rem(col + o, e)
        slot = lax.rem(col + e - each * (to // each), e)
        start(remote(xs.at[to], xr.at[slot], x_s.at[o], x_r.at[o], {"expert": to}))
    xr[lax.rem(col + e - shift, e)] = xs[col]
    for o in range(1, e):
        src = lax.rem(col + e - o, e)
        slot = lax.rem(src + e - shift, e)
        remote(xs.at[0], xr.at[slot], x_s.at[o], x_r.at[o], {"expert": src}).wait_recv()

    for j, (low, high) in enumerate(spans()):
        rows = lax.broadcasted_iota(jnp.int32, (1, high - low, features), 1) + low
        keep = jnp.logical_and(rows >= CAP * j, rows < CAP * (j + 1))
        xm[j][...] = jnp.where(keep, xr[:, low:high, :].astype(F32), 0.0).astype(BF16)
    w1.wait()
    group = min(4, e)

    def partial(gq, dst, d):
        for side in range(2):
            lanes = pl.ds(pl.multiple_of(side * ff + gq * quarter, 128), quarter)

            def body(i, carry):
                own = pl.ds(i * group, group)
                tiles = {}
                for j, (low, high) in enumerate(spans()):
                    left_side = xm[j][own].reshape(group * (high - low), features)
                    y = jnp.dot(left_side, wg[j, :, lanes], preferred_element_type=F32)
                    y = y.reshape(group, high - low, quarter)
                    for tile in range(low // TILE, high // TILE):
                        piece = y[:, tile * TILE - low:(tile + 1) * TILE - low, :]
                        tiles[tile] = piece if tile not in tiles else tiles[tile] + piece
                for tile, value in tiles.items():
                    dst[d, own, tile * TILE:(tile + 1) * TILE, side * quarter:(side + 1) * quarter] = (
                        value.astype(BF16)
                    )
                return carry

            lax.fori_loop(0, e // group, body, 0)

    def chunk(d, t):
        return lax.rem(z + (chips + chips - 1 - t if d == 0 else 1 + t), chips)

    def blocks(ref, d, k):
        return ref.at[d, pl.ds(k * each, each)]

    for d in range(2):
        partial(2 * other + d, psib, d)
        for t in range(chips):
            k = chunk(d, t)
            start(remote(blocks(psib, d, k), blocks(rsib, d, k), sib_s.at[d, t], sib_r.at[d, t], sibling))

    def sib_wait(d, t):
        k = chunk(d, t)
        remote(blocks(psib, d, k), blocks(rsib, d, k), sib_s.at[d, t], sib_r.at[d, t], sibling).wait_recv()

    def hop(d, t, u):
        b = chunk(d, t) * each + u
        return remote(pown.at[d, b], rr.at[d, t, u], rs_s.at[d, t, u], rs_r.at[d, t, u], ways[d])

    for d in range(2):
        partial(2 * c + d, pown, d)
        sib_wait(d, 0)
        for u in range(each):
            b = chunk(d, 0) * each + u
            pown[d, b] = (pown[d, b].astype(F32) + rsib[d, b].astype(F32)).astype(BF16)
            hop(d, 0, u).start()

    def ring(t, carry):
        for d in range(2):
            sib_wait(d, t)
        for u in range(each):
            for d in range(2):
                b = chunk(d, t) * each + u
                hop(d, t - 1, u).wait_recv()
                value = pown[d, b].astype(F32) + rsib[d, b].astype(F32) + rr[d, t - 1, u].astype(F32)
                pown[d, b] = value.astype(BF16)
                hop(d, t, u).start()
        return carry

    lax.fori_loop(1, chips - 1, ring, 0)
    for d in range(2):
        sib_wait(d, chips - 1)
    for u in range(each):
        b = z * each + u
        for d in range(2):
            hop(d, chips - 2, u).wait_recv()
            value = pown[d, b].astype(F32) + rsib[d, b].astype(F32) + rr[d, chips - 2, u].astype(F32)
            gate = value[:, :quarter]
            act[c, b, :, d * quarter:(d + 1) * quarter] = (
                gate / (1.0 + jnp.exp(-gate)) * value[:, quarter:]
            ).astype(BF16)

    def goes(t, d, u):
        return t < half - 1 or (t == half - 1 and u % 2 == d)

    def spread(d, t, u, b):
        return remote(act.at[c, b], act.at[c, b], ag_s.at[d, t, u], ag_r.at[d, t, u], ways[d])

    def hand(core, sem, b):
        return remote(act.at[core, b], act.at[core, b], fw_s.at[sem], fw_r.at[sem], sibling)

    def code(d, t, u):
        return (t * 2 + d) * each + u

    for u in range(each):
        b = z * each + u
        for d in range(2):
            if goes(0, d, u):
                start(spread(d, 0, u, b))
        mine = remote(act.at[c, b], act.at[c, b], me_sem.at[0, u], me_sem.at[1, u], sibling)
        start(mine)
    w2.wait()

    def finish(slots):
        pieces = [None] * (unit // TILE)
        count = len(slots)
        for j, (low, high) in enumerate(spans()):
            tall = high - low
            y = None
            for core in range(2):
                lhs = jnp.concatenate([act[core, b, low:high, :] for b in slots], axis=0)
                term = jnp.dot(
                    lhs, wd[j, core * 2 * quarter:(core + 1) * 2 * quarter, :], preferred_element_type=F32
                )
                y = term if y is None else y + term
            for tile in range(low // TILE, high // TILE):
                rows = lax.broadcasted_iota(jnp.int32, (TILE, 1), 0) + tile * TILE
                keep = jnp.logical_and(rows >= CAP * j, rows < CAP * (j + 1))
                got = []
                for i in range(count):
                    first = i * tall + tile * TILE - low
                    got.append(jnp.where(keep, y[first:first + TILE, :], 0.0))
                if pieces[tile] is None:
                    pieces[tile] = got
                else:
                    pieces[tile] = [p + g for p, g in zip(pieces[tile], got)]
        for i, b in enumerate(slots):
            for tile in range(unit // TILE):
                osend[b, tile * TILE:(tile + 1) * TILE, :] = pieces[tile][i].astype(BF16)
            target = lax.rem(b + shift, e)

            @pl.when(target != col)
            def _():
                remote(osend.at[b], oret.at[col], o_s.at[b], o_r.at[col], {"expert": target}).start()

            @pl.when(target == col)
            def _():
                oret[col] = osend[b]

    pending = []
    for u in range(each):
        b = z * each + u
        pending.append(
            (b, remote(act.at[other, b], act.at[other, b], me_sem.at[0, u], me_sem.at[1, u], sibling))
        )
    for t in range(half):
        arrived = []
        for u in range(each):
            for d in range(2):
                if not goes(t, d, u):
                    continue
                k = lax.rem(z + (chips - 1 - t if d == 0 else 1 + t), chips)
                b = k * each + u
                spread(d, t, u, b).wait_recv()
                if goes(t + 1, d, u):
                    start(spread(d, t + 1, u, b))
                start(hand(c, code(d, t, u), b))
                arrived.append((b, hand(other, code(d, t, u), b)))
        for b, copy in pending:
            copy.wait_recv()
        finish([b for b, copy in pending])
        pending = arrived
    for b, copy in pending:
        copy.wait_recv()
    finish([b for b, copy in pending])

    for o in range(1, e):
        src = lax.rem(col + o, e)
        remote(osend.at[0], oret.at[src], o_s.at[0], o_r.at[src], {"expert": src}).wait_recv()
    returned = oret[...].reshape(e * unit, out.shape[1])
    total = jnp.dot(chi[...], returned, preferred_element_type=F32)
    total = total + jnp.dot(clo[...], returned, preferred_element_type=F32)
    out[...] = total.astype(BF16)

    for copy in sent:
        copy.wait_send()

    def drain(t, carry):
        for d in range(2):
            for u in range(each):
                hop(d, t, u).wait_send()
        return carry

    lax.fori_loop(0, chips - 1, drain, 0)

    def drain_out(b, carry):
        target = lax.rem(b + shift, e)

        @pl.when(target != col)
        def _():
            remote(osend.at[b], oret.at[col], o_s.at[b], o_r.at[col], {"expert": target}).wait_send()

        return carry

    lax.fori_loop(0, e, drain_out, 0)


def on_device(
    n, e, queries, prompt_kv, gen_kv, gen_lengths, out_proj, residual, norm_gain,
    w_gate_up, w_down, routes, route_probs,
):
    prompts = queries.shape[0]
    rows = prompts * n
    features = residual.shape[2]
    chips = n // 2
    half = chips // 2
    each = e // chips
    topk = routes.shape[2]
    experts = EXP_COL * e
    unit = -(-EXP_COL * CAP // TILE) * TILE

    ids = routes.reshape(rows, topk)
    probs = route_probs.reshape(rows, topk)
    named = ids[:, :, None] == jnp.arange(experts, dtype=jnp.int32)[None, None, :]
    hits = jnp.sum(named.astype(F32), axis=1)
    weight = jnp.sum(jnp.where(named, probs[:, :, None], 0.0), axis=1)
    earlier = (jnp.arange(rows)[:, None] > jnp.arange(rows)[None, :]).astype(BF16)
    before = jnp.dot(earlier, hits.astype(BF16), preferred_element_type=F32)
    place = jnp.where(hits > 0, before, -1.0)
    slots = jnp.arange(CAP, dtype=F32)
    is_slot = place.T.reshape(e, EXP_COL, 1, rows) == slots[None, None, :, None]
    spare = ((0, 0), (0, unit - EXP_COL * CAP), (0, 0))
    pick = jnp.pad(is_slot.astype(BF16).reshape(e, EXP_COL * CAP, rows), spare).reshape(e * unit, rows)
    mix = jnp.where(
        place.reshape(rows, e, EXP_COL, 1) == slots[None, None, None, :],
        weight.reshape(rows, e, EXP_COL, 1),
        0.0,
    ).reshape(rows, e, EXP_COL * CAP)
    mix = jnp.pad(mix, ((0, 0), (0, 0), (0, unit - EXP_COL * CAP))).reshape(rows, e * unit)
    high = lax.reduce_precision(mix, 8, 7)
    chi = high.astype(BF16)
    clo = (mix - high).astype(BF16)

    heads = queries.shape[2] // HDIM
    lens = jnp.broadcast_to(gen_lengths.astype(BF16)[:, :, None, None], (prompts, 2, GROUPS, HDIM))
    q = jnp.concatenate([queries.reshape(prompts, 2, heads // 2, HDIM), lens], axis=2)
    width = HEADS_HERE * GROUPS * HDIM
    wide = HEADS_HERE * HDIM
    tokens, gen = prompt_kv.shape[1], gen_kv.shape[2]
    anywhere = pl.BlockSpec(memory_space=pl.ANY)
    vmem = pl.BlockSpec(memory_space=pltpu.VMEM)
    dma = pltpu.SemaphoreType.DMA
    mixed, normed = pl.pallas_call(
        functools.partial(attend_kernel, n),
        out_shape=(jax.ShapeDtypeStruct((rows, features), BF16), jax.ShapeDtypeStruct((rows, features), BF16)),
        in_specs=[anywhere] * 4 + [vmem] * 2,
        out_specs=(vmem, vmem),
        scratch_shapes=[
            pltpu.VMEM((n, 3 * GROUPS, HDIM), BF16),
            pltpu.VMEM((n, tokens, wide), BF16),
            pltpu.VMEM((n, tokens, wide), BF16),
            pltpu.VMEM((n, gen, wide), BF16),
            pltpu.VMEM((n, gen, wide), BF16),
            pltpu.VMEM((2, width, features), BF16),
            pltpu.VMEM((HEADS_HERE, n * GROUPS, HDIM), BF16),
            pltpu.VMEM((2, rows, width), BF16),
            pltpu.VMEM((8, rows), F32),
            pltpu.VMEM((n, 8, rows), F32),
            dma((6,)),
            dma((5, n)),
            dma((5, n)),
            dma((2, half, 2)),
            dma((2, half, 2)),
            dma((2, half, 2)),
            dma((2, half, 2)),
            dma((2,)),
            dma((n,)),
            dma((n,)),
        ],
        compiler_params=pltpu.CompilerParams(
            collective_id=0, has_side_effects=True, vmem_limit_bytes=40 << 20
        ),
        name="attend",
    )(
        q,
        prompt_kv,
        gen_kv.reshape(prompts, gen, gen_kv.shape[3]),
        out_proj.reshape(2, width, features),
        residual.reshape(rows, features),
        norm_gain.reshape(1, features),
    )

    quarter = w_gate_up.shape[2] // 8
    out_features = w_down.shape[2]
    band = spans()
    expert_out = pl.pallas_call(
        functools.partial(expert_kernel, n, e),
        out_shape=jax.ShapeDtypeStruct((rows, out_features), BF16),
        in_specs=[vmem] * 4 + [anywhere] * 2,
        out_specs=vmem,
        scratch_shapes=[
            pltpu.VMEM((e, unit, features), BF16),
            pltpu.VMEM((e, unit, features), BF16),
        ]
        + [pltpu.VMEM((e, top - low, features), BF16) for low, top in band]
        + [
            pltpu.VMEM(w_gate_up.shape, BF16),
            pltpu.VMEM(w_down.shape, BF16),
            pltpu.VMEM((2, e, unit, 2 * quarter), BF16),
            pltpu.VMEM((2, e, unit, 2 * quarter), BF16),
            pltpu.VMEM((2, e, unit, 2 * quarter), BF16),
            pltpu.VMEM((2, chips - 1, each, unit, 2 * quarter), BF16),
            pltpu.VMEM((2, e, unit, 2 * quarter), BF16),
            pltpu.VMEM((e, unit, out_features), BF16),
            pltpu.VMEM((e, unit, out_features), BF16),
            dma((2,)),
            dma((e,)),
            dma((e,)),
            dma((2, chips)),
            dma((2, chips)),
            dma((2, chips - 1, each)),
            dma((2, chips - 1, each)),
            dma((2, half, each)),
            dma((2, half, each)),
            dma((2 * half * each,)),
            dma((2 * half * each,)),
            dma((2, each)),
            dma((e,)),
            dma((e,)),
        ],
        compiler_params=pltpu.CompilerParams(
            collective_id=1, has_side_effects=True, vmem_limit_bytes=56 << 20
        ),
        name="experts",
    )(normed, pick, chi, clo, w_gate_up, w_down)
    shape = (prompts, n, features)
    return (mixed.reshape(shape), expert_out.reshape(shape))


def solution(mesh):
    placed = (
        P("expert", "sample", None),
        P("expert", "sample", None),
        P("expert", "sample", None, None),
        P("expert", "sample"),
        P(None, "sample"),
        P("expert", None, "sample"),
        P("sample"),
        P("expert", "sample", None),
        P("expert", None, "sample"),
        P("expert", None, None),
        P("expert", None, None),
    )
    return jax.shard_map(
        functools.partial(on_device, mesh.shape["sample"], mesh.shape["expert"]),
        mesh=mesh,
        in_specs=placed,
        out_specs=(P("expert", None, "sample"), P("expert", None, "sample")),
        check_vma=False,
    )
```

```python
import functools

import jax
import jax.numpy as jnp
from jax import lax
from jax.experimental import pallas as pl
from jax.experimental.pallas import tpu as pltpu
from jax.sharding import PartitionSpec as P

MESH = pl.DeviceIdType.MESH
HDIM = 128
GROUPS = 16
KVHEADS = 4
HERE = 2
EXP_COL = 3
CAP = 26
TILE = 16
PIECES = 4
NEGATIVE = -1e30
EPSILON = 1e-06
F32 = jnp.float32
BF16 = jnp.bfloat16
NT = (((1,), (1,)), ((), ()))


def remote(src, dst, send, recv, device):
    return pltpu.make_async_remote_copy(
        src_ref=src, dst_ref=dst, send_sem=send, recv_sem=recv, device_id=device, device_id_type=MESH
    )


def spans():
    out = []
    for j in range(EXP_COL):
        low = CAP * j // TILE * TILE
        high = -(-CAP * (j + 1) // TILE) * TILE
        out.append((low, high))
    return out


def merge_tile(tile, parts):
    if len(parts) == 1:
        return parts[0][1]
    (first, a), (second, b) = parts
    shape = (1,) * (a.ndim - 2) + (TILE, 1)
    rows = lax.broadcasted_iota(jnp.int32, shape, a.ndim - 2) + tile * TILE
    return jnp.where(rows < CAP * (first + 1), a, b)


def token_order(chips):
    return [0] + sorted(range(1, chips), key=lambda d: -min(d, chips - d))


def kernel(
    n, e,
    q, lens, kv, gkv, wo, res, gain, ids, probs, wgu, wdn,
    mixed, out,
    kvv, gv, gmsg, rq, rm, rk, rv, wov, wg, wd, ost, mst, lst, obuf, att, sqs, sqr,
    place, pick, chi, clo, y, xs, xr, pown, psib, rsib, rr, act, osend, oret, fsend, frecv,
    lsem, ex_s, ex_r, ag_s, ag_r, sib_s, sib_r, own_sem, sq_ss, sq_rs,
    x_s, x_r, ps_s, ps_r, rs_s, rs_r, aa_s, aa_r, fw_s, fw_r, me_sem, o_s, o_r, f_s, f_r,
):
    chips = n // 2
    half = chips // 2
    each = e // chips
    me = lax.axis_index("sample")
    col = lax.axis_index("expert")
    z, c = me // 2, lax.rem(me, 2)
    other = 1 - c
    wide = HERE * HDIM
    right = {"sample": 2 * lax.rem(z + 1, chips) + c}
    left = {"sample": 2 * lax.rem(z + chips - 1, chips) + c}
    ways = (right, left)
    sibling = {"sample": 2 * z + other}
    unit = xs.shape[1]
    rows_all, features = res.shape
    sent = []

    def start(copy):
        copy.start()
        sent.append(copy)

    def fetch(src, dst, k):
        copy = pltpu.make_async_copy(src, dst, lsem.at[k])
        copy.start()
        return copy

    fetch_g = fetch(gkv, gv, 1)
    fetch_kv = fetch(kv, kvv, 2)

    barrier = pltpu.get_barrier_semaphore()

    def greet_sample(o, carry):
        pl.semaphore_signal(barrier, inc=1, device_id={"sample": lax.rem(me + o, n)}, device_id_type=MESH)
        return carry

    def greet_expert(o, carry):
        pl.semaphore_signal(barrier, inc=1, device_id={"expert": lax.rem(col + o, e)}, device_id_type=MESH)
        return carry

    lax.fori_loop(1, n, greet_sample, 0)
    lax.fori_loop(1, e, greet_expert, 0)

    fetch_g.wait()
    prompts = q.shape[0]
    gen = gv.shape[1]
    scale = HDIM ** (-0.5)
    tall = prompts * GROUPS
    length = jnp.broadcast_to(lens[...], (prompts, GROUPS, HDIM)).reshape(tall, HDIM)[:, 0:1]
    lane = lax.broadcasted_iota(jnp.int32, (tall, HDIM), 1)
    for hp in range(2):
        stats = jnp.zeros((tall, HDIM), F32)
        for hl in range(HERE):
            h = hp * HERE + hl
            query = q[:, h * GROUPS:(h + 1) * GROUPS, :].reshape(tall, HDIM)
            keys = gv[:, :, h * HDIM:(h + 1) * HDIM].reshape(prompts * gen, HDIM)
            vals = gv[:, :, (KVHEADS + h) * HDIM:(KVHEADS + h + 1) * HDIM].reshape(prompts * gen, HDIM)
            scores = lax.dot_general(query, keys, NT, preferred_element_type=F32) * scale
            row = lax.broadcasted_iota(jnp.int32, scores.shape, 0) // GROUPS
            at_key = (lax.broadcasted_iota(jnp.int32, scores.shape, 1) - row * gen).astype(F32)
            scores = jnp.where(jnp.logical_and(at_key >= 0.0, at_key < length), scores, NEGATIVE)
            highest = jnp.max(scores, axis=1, keepdims=True)
            weight = jnp.exp(scores - highest)
            total = jnp.sum(weight, axis=1, keepdims=True)
            got = jnp.dot(weight.astype(BF16), vals, preferred_element_type=F32) / total
            gmsg[:, hp, hl * GROUPS:(hl + 1) * GROUPS, :] = got.astype(BF16).reshape(prompts, GROUPS, HDIM)
            level = highest + jnp.log(total)
            for k in range(3):
                part = level.astype(BF16).astype(F32)
                level = level - part
                stats = jnp.where(lane == 3 * hl + k, part, stats)
        gmsg[:, hp, HERE * GROUPS:, :] = stats.astype(BF16).reshape(prompts, GROUPS, HDIM)
    fetch_kv.wait()

    pl.semaphore_wait(barrier, n - 1 + e - 1)

    order = token_order(chips)
    where_of = {d: i for i, d in enumerate(order)}

    def q_pair(p, hp):
        return q.at[p, pl.ds(pl.multiple_of(hp * HERE * GROUPS, HERE * GROUPS), HERE * GROUPS)], rq.at[me]

    def m_pair(p, hp):
        return gmsg.at[p, hp], rm.at[me]

    def k_pair(p, hp, slot):
        return kvv.at[p, :, pl.ds(pl.multiple_of(hp * wide, wide), wide)], rk.at[slot]

    def v_pair(p, hp, slot):
        return kvv.at[p, :, pl.ds(pl.multiple_of((2 + hp) * wide, wide), wide)], rv.at[slot]

    def exchange(kind, dz, hp):
        p = lax.rem(z + dz, chips)
        slot = 2 * where_of[(chips - dz) % chips] + c
        src, dst = (
            q_pair(p, hp), m_pair(p, hp), k_pair(p, hp, slot), v_pair(p, hp, slot)
        )[kind]
        target = {"sample": 2 * p + hp}
        start(remote(src, dst, ex_s.at[kind, 2 * dz + (hp if dz else 0)], ex_r.at[kind, slot], target))

    for kind in range(2):
        for dz in order[1:]:
            for hp in range(2):
                exchange(kind, dz, hp)
        exchange(kind, 0, other)
    exchange(2, 0, other)
    exchange(3, 0, other)
    for dz in order[1:]:
        for hp in range(2):
            exchange(2, dz, hp)
            exchange(3, dz, hp)
    local = []
    for kind, (src, dst) in enumerate((q_pair(z, c), m_pair(z, c), k_pair(z, c, c), v_pair(z, c, c))):
        local.append(fetch(src, dst, kind))
    fetch_wo = fetch(wo, wov, 4)
    fetch_wg = fetch(wgu, wg, 5)
    fetch_wd = fetch(wdn, wd, 6)

    experts = place.shape[1]
    topk = ids.shape[1]
    named = jnp.zeros((topk, rows_all), F32)
    given = jnp.zeros((topk, rows_all), F32)
    for p in range(prompts):
        sample = lax.broadcasted_iota(jnp.int32, (n, rows_all), 0)
        there = lax.broadcasted_iota(jnp.int32, (n, rows_all), 1) == sample + p * n
        there = jnp.where(there, 1.0, 0.0).astype(BF16)
        named = named + jnp.dot(ids[p].astype(F32).astype(BF16), there, preferred_element_type=F32)
        rest = probs[p]
        for k in range(3):
            part = rest.astype(BF16)
            rest = rest - part.astype(F32)
            given = given + jnp.dot(part, there, preferred_element_type=F32)
    lane = lax.broadcasted_iota(jnp.int32, (rows_all, experts), 1)
    expert_row = lax.broadcasted_iota(jnp.int32, (experts, rows_all), 0).astype(F32)
    hits = jnp.zeros((experts, rows_all), F32)
    share_t = jnp.zeros((experts, rows_all), F32)
    for k in range(topk):
        same = expert_row == named[k:k + 1, :]
        hits = hits + jnp.where(same, 1.0, 0.0)
        share_t = share_t + jnp.where(same, given[k:k + 1, :], 0.0)
    square = (rows_all, rows_all)
    row_index = lax.broadcasted_iota(jnp.int32, square, 0)
    lane_index = lax.broadcasted_iota(jnp.int32, square, 1)
    above = jnp.where(row_index < lane_index, 1.0, 0.0).astype(BF16)
    eye_bf = jnp.where(row_index == lane_index, 1.0, 0.0).astype(BF16)
    before = jnp.dot(hits.astype(BF16), above, preferred_element_type=F32)
    place_t = jnp.where(hits > 0.5, before, -1.0).astype(BF16)
    place[...] = lax.dot_general(eye_bf, place_t, NT, preferred_element_type=F32).astype(BF16)
    at = lax.broadcasted_iota(jnp.int32, (e, unit, experts), 1)
    local_expert = jnp.zeros((e, unit, experts), jnp.int32)
    for j in range(1, EXP_COL):
        local_expert = local_expert + jnp.where(at >= CAP * j, 1, 0)
    slot_of = (at - CAP * local_expert).astype(F32)
    owner = lax.broadcasted_iota(jnp.int32, (e, unit, experts), 0) * EXP_COL + local_expert
    on_lane = lax.broadcasted_iota(jnp.int32, (e, unit, experts), 2)
    table = jnp.where(owner == on_lane, 1.0, 0.0).astype(BF16).reshape(e * unit, experts)
    seen = jnp.dot(table, place_t, preferred_element_type=F32)
    pick[...] = jnp.where(seen.reshape(e, unit, rows_all) == slot_of[:, :, :rows_all], 1.0, 0.0).astype(BF16)
    slot_table = jnp.where(on_lane == 0, slot_of, 0.0).astype(BF16).reshape(e * unit, experts)
    first_lane = jnp.where(lane == 0, 1.0, 0.0).astype(BF16)
    slot_row = lax.dot_general(first_lane, slot_table, NT, preferred_element_type=F32)
    placed = lax.dot_general(place[...], table, NT, preferred_element_type=F32)
    chosen = placed == slot_row
    for k, ref in enumerate((chi, clo)):
        part_t = share_t.astype(BF16)
        share_t = share_t - part_t.astype(F32)
        part = lax.dot_general(eye_bf, part_t, NT, preferred_element_type=F32).astype(BF16)
        spread_part = lax.dot_general(part, table, NT, preferred_element_type=F32)
        ref[...] = jnp.where(chosen, spread_part, 0.0).astype(BF16)

    for copy in local:
        copy.wait()

    def arrived(kind, slot):
        if kind == 0:
            src, dst = q_pair(0, 0)
        elif kind == 1:
            src, dst = m_pair(0, 0)
        elif kind == 2:
            src, dst = k_pair(0, 0, slot)
        else:
            src, dst = v_pair(0, 0, slot)
        remote(src, dst, ex_s.at[kind, 1], ex_r.at[kind, slot], sibling).wait_recv()

    def arrive_all(kinds, low, high):
        def body(i, carry):
            for kind in kinds:
                arrived(kind, i)
            return carry

        lax.fori_loop(low, high, body, 0)

    for kind in range(4):
        arrived(kind, other)
    arrive_all((0, 1), 2, n)
    first = n // 2
    arrive_all((2, 3), 2, first)
    block = min(8, n)
    slab = block * GROUPS

    def absorb(h, i, low, high, highest, total, acc):
        own = pl.ds(i * block, block)
        query = rq[own, h * GROUPS:(h + 1) * GROUPS, :].reshape(slab, HDIM)
        lanes = slice(h * HDIM, (h + 1) * HDIM)
        count = (high - low) * rk.shape[1]
        keys = rk[low:high, :, lanes].reshape(count, HDIM)
        vals = rv[low:high, :, lanes].reshape(count, HDIM)
        scores = lax.dot_general(query, keys, NT, preferred_element_type=F32) * scale
        peak = jnp.maximum(highest, jnp.max(scores, axis=1, keepdims=True))
        kept = jnp.exp(highest - peak)
        weight = jnp.exp(scores - peak)
        total = total * kept + jnp.sum(weight, axis=1, keepdims=True)
        acc = acc * kept + jnp.dot(weight.astype(BF16), vals, preferred_element_type=F32)
        return peak, total, acc

    def slab_rows(i):
        return pl.ds(pl.multiple_of(i * slab, slab), slab)

    for h in range(HERE):

        def stage_one(i, carry, h=h):
            own = pl.ds(i * block, block)
            stats = rm[own, HERE * GROUPS:, :].reshape(slab, HDIM).astype(F32)
            level = stats[:, 3 * h:3 * h + 1] + stats[:, 3 * h + 1:3 * h + 2] + stats[:, 3 * h + 2:3 * h + 3]
            acc = rm[own, h * GROUPS:(h + 1) * GROUPS, :].reshape(slab, HDIM).astype(F32)
            peak, total, acc = absorb(h, i, 0, first, level, jnp.ones((slab, 1), F32), acc)
            mst[h, slab_rows(i), :] = jnp.broadcast_to(peak, (slab, HDIM))
            lst[h, slab_rows(i), :] = jnp.broadcast_to(total, (slab, HDIM))
            ost[h, slab_rows(i), :] = acc
            return carry

        lax.fori_loop(0, n // block, stage_one, 0)

    count = n * GROUPS
    r = lax.broadcasted_iota(jnp.int32, (count, count), 0)
    k = lax.broadcasted_iota(jnp.int32, (count, count), 1)
    swap = jnp.where(k == (lax.rem(r, n) * GROUPS + r // n), 1.0, 0.0).astype(BF16)
    at_rows = pl.ds(pl.multiple_of(z * n, n), n)
    width = HERE * GROUPS * HDIM
    cut = width // PIECES
    per_head = PIECES // HERE

    def part(core, b, u):
        return att.at[core, pl.ds(pl.multiple_of(b * n, n), n), u * cut:(u + 1) * cut]

    def goes(t, d, u):
        return t < half - 1 or (t == half - 1 and u % 2 == d)

    def ring_block(t, d):
        return lax.rem(z + (chips - 1 - t if d == 0 else 1 + t), chips)

    def along(t, d, u, b):
        ref = part(c, b, u)
        return remote(ref, ref, ag_s.at[d, t, u], ag_r.at[d, t, u], ways[d])

    def across(core, t, d, u, b):
        ref = part(core, b, u)
        return remote(ref, ref, sib_s.at[d, t, u], sib_r.at[d, t, u], sibling)

    def own_across(core, u):
        ref = part(core, z, u)
        return remote(ref, ref, own_sem.at[0, u], own_sem.at[1, u], sibling)

    arrive_all((2, 3), first, n)
    for h in range(HERE):

        def stage_two(i, carry, h=h):
            peak = mst[h, slab_rows(i), 0:1]
            total = lst[h, slab_rows(i), 0:1]
            peak, total, acc = absorb(h, i, first, n, peak, total, ost[h, slab_rows(i), :])
            obuf[h, slab_rows(i), :] = (acc / total).astype(BF16)
            return carry

        lax.fori_loop(0, n // block, stage_two, 0)
        swapped = jnp.dot(swap, obuf[h], preferred_element_type=F32).astype(BF16)
        for g in range(GROUPS):
            begin = (h * GROUPS + g) * HDIM
            att[c, at_rows, begin:begin + HDIM] = swapped[g * n:(g + 1) * n, :]
        for u in range(h * per_head, (h + 1) * per_head):
            for d in range(2):
                if goes(0, d, u):
                    start(along(0, d, u, z))
        for u in range(h * per_head, (h + 1) * per_head):
            start(own_across(c, u))

    fetch_wo.wait()
    projected = jnp.zeros((rows_all, features), F32)

    def project(acc, core, u):
        lanes = slice(u * cut, (u + 1) * cut)
        return acc + jnp.dot(att[core, :, lanes], wov[core, lanes, :], preferred_element_type=F32)

    for t in range(half):
        for u in range(PIECES):
            for d in range(2):
                if not goes(t, d, u):
                    continue
                b = ring_block(t, d)
                along(t, d, u, b).wait_recv()
                if goes(t + 1, d, u):
                    start(along(t + 1, d, u, b))
                start(across(c, t, d, u, b))
            if t == half - 1:
                projected = project(projected, c, u)
    for u in range(PIECES):
        own_across(other, u).wait_recv()
        for t in range(half):
            for d in range(2):
                if goes(t, d, u):
                    across(other, t, d, u, ring_block(t, d)).wait_recv()
        projected = project(projected, other, u)

    mixed[...] = projected.astype(BF16)
    stream = res[...].astype(F32) + projected
    y[...] = (stream * gain[...]).astype(BF16)
    xs[...] = (
        jnp.dot(pick[...].reshape(e * unit, rows_all), y[...], preferred_element_type=F32)
        .astype(BF16)
        .reshape(e, unit, features)
    )

    shift = each * (col // each)

    def target_of(k, i):
        return each * lax.rem(col // each + chips + chips - k, chips) + i

    def slot_at(k):
        return k * each + lax.rem(col, each)

    chunks = []
    for t in range(half):
        for d in range(2):
            if t < half - 1 or d == 0:
                chunks.append(ring_block(t, d))
    chunks.append(z)
    for k in chunks:
        for i in range(each):
            to = target_of(k, i)

            @pl.when(to != col)
            def _(k=k, to=to):
                remote(xs.at[to], xr.at[slot_at(k)], x_s.at[to], x_r.at[slot_at(k)], {"expert": to}).start()

            @pl.when(to == col)
            def _(k=k, to=to):
                xr[slot_at(k)] = xs[to]

    def wait_rows(k):
        for i in range(each):
            b = k * each + i
            src = lax.rem(b + shift, e)

            @pl.when(src != col)
            def _(b=b, src=src):
                remote(xs.at[0], xr.at[b], x_s.at[0], x_r.at[b], {"expert": src}).wait_recv()

    eye = lax.broadcasted_iota(jnp.int32, square, 0) == lax.broadcasted_iota(jnp.int32, square, 1)
    column = jnp.sum(stream * stream, axis=1, keepdims=True)
    flat = jnp.sum(jnp.where(eye, column, 0.0), axis=0, keepdims=True)
    sqs[...] = jnp.broadcast_to(flat, sqs.shape)
    for o in range(1, n):
        start(remote(sqs, sqr.at[o], sq_ss.at[o], sq_rs.at[o], {"sample": lax.rem(me + o, n)}))

    quarter = pown.shape[3] // 2
    ff = 4 * quarter
    fetch_wg.wait()

    def chunk(d, t):
        return lax.rem(z + (chips + chips - 1 - t if d == 0 else 1 + t), chips)

    def partial(gq, dst, d, k):
        own = pl.ds(k * each, each)
        for side in range(2):
            lanes = pl.ds(pl.multiple_of(side * ff + gq * quarter, 128), quarter)
            tiles = {}
            for j, (low, high) in enumerate(spans()):
                lhs = xr[own, low:high, :].reshape(each * (high - low), features)
                got = jnp.dot(lhs, wg[j, :, lanes], preferred_element_type=F32)
                got = got.reshape(each, high - low, quarter)
                for tile in range(low // TILE, high // TILE):
                    piece = got[:, tile * TILE - low:(tile + 1) * TILE - low, :]
                    tiles.setdefault(tile, []).append((j, piece))
            for tile, parts in tiles.items():
                dst[d, own, tile * TILE:(tile + 1) * TILE, side * quarter:(side + 1) * quarter] = (
                    merge_tile(tile, parts).astype(BF16)
                )

    def pair(d, t):
        own = pl.ds(chunk(d, t) * each, each)
        return remote(psib.at[d, own], rsib.at[d, own], ps_s.at[d, t], ps_r.at[d, t], sibling)

    def hop(d, t, u):
        b = chunk(d, t) * each + u
        return remote(pown.at[d, b], rr.at[d, t, u], rs_s.at[d, t, u], rs_r.at[d, t, u], ways[d])

    def prepare(t):
        for d in range(2):
            partial(2 * other + d, psib, d, chunk(d, t))
            pair(d, t).start()
        for d in range(2):
            partial(2 * c + d, pown, d, chunk(d, t))

    def norm_factor():
        squares = sqs[...]
        for o in range(1, n):
            remote(
                sqs, sqr.at[o], sq_ss.at[o], sq_rs.at[o], {"sample": lax.rem(me + n - o, n)}
            ).wait_recv()
            squares = squares + sqr[o]
        factor = lax.rsqrt(squares / (features * n) + EPSILON)[0:1, :]
        for i in range(each):
            to = target_of(z, i)
            values = jnp.sum(pick[to].astype(F32) * factor, axis=1, keepdims=True)
            fsend[i] = jnp.broadcast_to(values, fsend.shape[1:])

            @pl.when(to != col)
            def _(i=i, to=to):
                place_at = lax.rem(col, each)
                remote(fsend.at[i], frecv.at[place_at], f_s.at[i], f_r.at[place_at], {"expert": to}).start()

            @pl.when(to == col)
            def _(i=i):
                frecv[lax.rem(col, each)] = fsend[i]

    def ring(t, carry):
        @pl.when(t < half)
        def _():
            wait_rows(chunk(0, t))

        @pl.when(t < half - 1)
        def _():
            wait_rows(chunk(1, t))

        prepare(t)
        for d in range(2):
            pair(d, t).wait_recv()
        for u in range(each):
            for d in range(2):
                b = chunk(d, t) * each + u

                @pl.when(t == 0)
                def _(d=d, b=b):
                    pown[d, b] = (pown[d, b].astype(F32) + rsib[d, b].astype(F32)).astype(BF16)

                @pl.when(t > 0)
                def _(d=d, b=b, u=u):
                    hop(d, t - 1, u).wait_recv()
                    value = pown[d, b].astype(F32) + rsib[d, b].astype(F32) + rr[d, t - 1, u].astype(F32)
                    pown[d, b] = value.astype(BF16)

                hop(d, t, u).start()

        @pl.when(t == 1)
        def _():
            norm_factor()

        return carry

    lax.fori_loop(0, chips - 1, ring, 0)
    wait_rows(z)
    prepare(chips - 1)
    for i in range(each):
        src = lax.rem(z * each + i + shift, e)

        @pl.when(src != col)
        def _(i=i, src=src):
            remote(fsend.at[0], frecv.at[i], f_s.at[0], f_r.at[i], {"expert": src}).wait_recv()

    for d in range(2):
        pair(d, chips - 1).wait_recv()

    def spread(d, t, u, b):
        return remote(act.at[c, b], act.at[c, b], aa_s.at[d, t, u], aa_r.at[d, t, u], ways[d])

    def hand(core, d, t, u, b):
        return remote(act.at[core, b], act.at[core, b], fw_s.at[d, t, u], fw_r.at[d, t, u], sibling)

    def own_hand(core, u):
        b = z * each + u
        return remote(act.at[core, b], act.at[core, b], me_sem.at[0, u], me_sem.at[1, u], sibling)

    for u in range(each):
        b = z * each + u
        factor = frecv[u][:, 0:1]
        for d in range(2):
            hop(d, chips - 2, u).wait_recv()
            value = pown[d, b].astype(F32) + rsib[d, b].astype(F32) + rr[d, chips - 2, u].astype(F32)
            value = value * factor
            gate = value[:, :quarter]
            act[c, b, :, d * quarter:(d + 1) * quarter] = (
                gate / (1.0 + jnp.exp(-gate)) * value[:, quarter:]
            ).astype(BF16)
        for d in range(2):
            if goes(0, d, u):
                start(spread(d, 0, u, b))
        start(own_hand(c, u))
    fetch_wd.wait()

    def finish(slots):
        tiles = {}
        count = len(slots)
        for j, (low, high) in enumerate(spans()):
            got = None
            for core in range(2):
                lhs = jnp.concatenate([act[core, b, low:high, :] for b in slots], axis=0)
                depth = slice(core * 2 * quarter, (core + 1) * 2 * quarter)
                term = jnp.dot(lhs, wd[j, depth, :], preferred_element_type=F32)
                got = term if got is None else got + term
            got = got.reshape(count, high - low, got.shape[1])
            for tile in range(low // TILE, high // TILE):
                piece = got[:, tile * TILE - low:(tile + 1) * TILE - low, :]
                tiles.setdefault(tile, []).append((j, piece))
        done = {tile: merge_tile(tile, parts).astype(BF16) for tile, parts in tiles.items()}
        for i, b in enumerate(slots):
            for tile, value in done.items():
                osend[b, tile * TILE:(tile + 1) * TILE, :] = value[i]
            target = lax.rem(b + shift, e)

            @pl.when(target != col)
            def _(b=b, target=target):
                remote(osend.at[b], oret.at[col], o_s.at[b], o_r.at[col], {"expert": target}).start()

            @pl.when(target == col)
            def _(b=b):
                oret[col] = osend[b]

    def complete(pending):
        for b, copy in pending:
            copy.wait_recv()
        finish([b for b, copy in pending])

    pending = [(z * each + u, own_hand(other, u)) for u in range(each)]
    for t in range(half):
        if t == half - 1:
            complete(pending)
            pending = []
        fresh = []
        for u in range(each):
            for d in range(2):
                if not goes(t, d, u):
                    continue
                b = ring_block(t, d) * each + u
                spread(d, t, u, b).wait_recv()
                if goes(t + 1, d, u):
                    start(spread(d, t + 1, u, b))
                start(hand(c, d, t, u, b))
                fresh.append((b, hand(other, d, t, u, b)))
        if pending:
            complete(pending)
        pending = fresh
    complete(pending)

    def wait_return(o, carry):
        src = lax.rem(col + o, e)
        remote(osend.at[0], oret.at[src], o_s.at[0], o_r.at[src], {"expert": src}).wait_recv()
        return carry

    lax.fori_loop(1, e, wait_return, 0)
    returned = oret[...].reshape(e * unit, out.shape[1])
    total = jnp.dot(chi[...], returned, preferred_element_type=F32)
    total = total + jnp.dot(clo[...], returned, preferred_element_type=F32)
    out[...] = total.astype(BF16)

    for copy in sent:
        copy.wait_send()

    def drain(t, carry):
        for d in range(2):
            pair(d, t).wait_send()

            @pl.when(t < chips - 1)
            def _(d=d):
                for u in range(each):
                    hop(d, t, u).wait_send()

        return carry

    lax.fori_loop(0, chips, drain, 0)

    def drain_out(b, carry):
        target = lax.rem(b + shift, e)

        @pl.when(target != col)
        def _():
            remote(osend.at[b], oret.at[col], o_s.at[b], o_r.at[col], {"expert": target}).wait_send()

        @pl.when(b != col)
        def _():
            remote(xs.at[b], xr.at[0], x_s.at[b], x_r.at[0], {"expert": b}).wait_send()

        return carry

    lax.fori_loop(0, e, drain_out, 0)
    for i in range(each):
        to = target_of(z, i)

        @pl.when(to != col)
        def _(i=i, to=to):
            remote(fsend.at[i], frecv.at[0], f_s.at[i], f_r.at[0], {"expert": to}).wait_send()


def on_device(
    n, e, queries, prompt_kv, gen_kv, gen_lengths, out_proj, residual, norm_gain,
    w_gate_up, w_down, routes, route_probs,
):
    prompts = queries.shape[0]
    rows = prompts * n
    features = residual.shape[2]
    out_features = w_down.shape[2]
    chips = n // 2
    half = chips // 2
    each = e // chips
    unit = -(-EXP_COL * CAP // TILE) * TILE
    heads = queries.shape[2] // HDIM
    width = HERE * GROUPS * HDIM
    wide = HERE * HDIM
    tokens, gen = prompt_kv.shape[1], gen_kv.shape[2]
    quarter = w_gate_up.shape[2] // 8
    table = 128
    hbm = pl.BlockSpec(memory_space=pltpu.HBM)
    vmem = pl.BlockSpec(memory_space=pltpu.VMEM)
    dma = pltpu.SemaphoreType.DMA
    buf = pltpu.VMEM
    lens = jnp.broadcast_to(gen_lengths.astype(F32)[:, :, None], (prompts, 1, HDIM))
    mixed, expert_out = pl.pallas_call(
        functools.partial(kernel, n, e),
        out_shape=(
            jax.ShapeDtypeStruct((rows, features), BF16),
            jax.ShapeDtypeStruct((rows, out_features), BF16),
        ),
        in_specs=[vmem, vmem, hbm, hbm, hbm, vmem, vmem, vmem, vmem, hbm, hbm],
        out_specs=(vmem, vmem),
        scratch_shapes=[
            buf(prompt_kv.shape, BF16),
            buf((prompts, gen, gen_kv.shape[3]), BF16),
            buf((prompts, 2, (HERE + 1) * GROUPS, HDIM), BF16),
            buf((n, HERE * GROUPS, HDIM), BF16),
            buf((n, (HERE + 1) * GROUPS, HDIM), BF16),
            buf((n, tokens, wide), BF16),
            buf((n, tokens, wide), BF16),
            buf((2, width, features), BF16),
            buf(w_gate_up.shape, BF16),
            buf(w_down.shape, BF16),
            buf((HERE, n * GROUPS, HDIM), F32),
            buf((HERE, n * GROUPS, HDIM), F32),
            buf((HERE, n * GROUPS, HDIM), F32),
            buf((HERE, n * GROUPS, HDIM), BF16),
            buf((2, rows, width), BF16),
            buf((8, rows), F32),
            buf((n, 8, rows), F32),
            buf((rows, table), BF16),
            buf((e, unit, rows), BF16),
            buf((rows, e * unit), BF16),
            buf((rows, e * unit), BF16),
            buf((rows, features), BF16),
            buf((e, unit, features), BF16),
            buf((e, unit, features), BF16),
            buf((2, e, unit, 2 * quarter), BF16),
            buf((2, e, unit, 2 * quarter), BF16),
            buf((2, e, unit, 2 * quarter), BF16),
            buf((2, chips - 1, each, unit, 2 * quarter), BF16),
            buf((2, e, unit, 2 * quarter), BF16),
            buf((e, unit, out_features), BF16),
            buf((e, unit, out_features), BF16),
            buf((each, unit, HDIM), F32),
            buf((each, unit, HDIM), F32),
            dma((7,)),
            dma((4, n)),
            dma((4, n)),
            dma((2, half, PIECES)),
            dma((2, half, PIECES)),
            dma((2, half, PIECES)),
            dma((2, half, PIECES)),
            dma((2, PIECES)),
            dma((n,)),
            dma((n,)),
            dma((e,)),
            dma((e,)),
            dma((2, chips)),
            dma((2, chips)),
            dma((2, chips - 1, each)),
            dma((2, chips - 1, each)),
            dma((2, half, each)),
            dma((2, half, each)),
            dma((2, half, each)),
            dma((2, half, each)),
            dma((2, each)),
            dma((e,)),
            dma((e,)),
            dma((each,)),
            dma((each,)),
        ],
        compiler_params=pltpu.CompilerParams(
            collective_id=0, has_side_effects=True, vmem_limit_bytes=53 << 20
        ),
        name="decode_step",
    )(
        queries.reshape(prompts, heads, HDIM),
        lens,
        prompt_kv,
        gen_kv.reshape(prompts, gen, gen_kv.shape[3]),
        out_proj.reshape(2, width, features),
        residual.reshape(rows, features),
        norm_gain.reshape(1, features),
        jnp.swapaxes(routes, 1, 2),
        jnp.swapaxes(route_probs, 1, 2),
        w_gate_up,
        w_down,
    )
    shape = (prompts, n, features)
    return (mixed.reshape(shape), expert_out.reshape(shape))


def solution(mesh):
    placed = (
        P("expert", "sample", None),
        P("expert", "sample", None),
        P("expert", "sample", None, None),
        P("expert", "sample"),
        P(None, "sample"),
        P("expert", None, "sample"),
        P("sample"),
        P("expert", "sample", None),
        P("expert", None, "sample"),
        P("expert", None, None),
        P("expert", None, None),
    )
    return jax.shard_map(
        functools.partial(on_device, mesh.shape["sample"], mesh.shape["expert"]),
        mesh=mesh,
        in_specs=placed,
        out_specs=(P("expert", None, "sample"), P("expert", None, "sample")),
        check_vma=False,
    )
```

```python
import functools

import jax
import jax.numpy as jnp
from jax import lax
from jax.experimental import pallas as pl
from jax.experimental.pallas import tpu as pltpu
from jax.sharding import PartitionSpec as P

MESH = pl.DeviceIdType.MESH
HDIM = 128
GROUPS = 16
KVHEADS = 4
HERE = 2
EXP_COL = 3
CAP = 26
TILE = 16
PIECES = 4
NEGATIVE = -1e30
EPSILON = 1e-06
F32 = jnp.float32
BF16 = jnp.bfloat16
NT = (((1,), (1,)), ((), ()))


def remote(src, dst, send, recv, device):
    return pltpu.make_async_remote_copy(
        src_ref=src, dst_ref=dst, send_sem=send, recv_sem=recv, device_id=device, device_id_type=MESH
    )


def spans():
    out = []
    for j in range(EXP_COL):
        low = CAP * j // TILE * TILE
        high = -(-CAP * (j + 1) // TILE) * TILE
        out.append((low, high))
    return out


def merge_tile(tile, parts):
    if len(parts) == 1:
        return parts[0][1]
    (first, a), (second, b) = parts
    shape = (1,) * (a.ndim - 2) + (TILE, 1)
    rows = lax.broadcasted_iota(jnp.int32, shape, a.ndim - 2) + tile * TILE
    return jnp.where(rows < CAP * (first + 1), a, b)


def token_order(chips):
    return [0] + sorted(range(1, chips), key=lambda d: -min(d, chips - d))


def kernel(
    n, e,
    q_in, lens_in, kv, gkv, wo, res_in, gain_in, ids_in, probs_in, wgu, wdn,
    mixed, out,
    qraw, qwide, q, lens, res, gain, ids, probs, kvv, gv, gmsg, rq, rm, rkv, wov, wg, wd, ost, mst, lst, obuf, att, sqs, sqr,
    place, pick, chi, clo, y, xs, xr, pown, psib, rsib, rr, act, osend, oret, fsend, frecv,
    lsem, ex_s, ex_r, ag_s, ag_r, sib_s, sib_r, own_sem, sq_ss, sq_rs,
    x_s, x_r, ps_s, ps_r, rs_s, rs_r, aa_s, aa_r, fw_s, fw_r, me_sem, o_s, o_r, f_s, f_r,
):
    chips = n // 2
    half = chips // 2
    each = e // chips
    me = lax.axis_index("sample")
    col = lax.axis_index("expert")
    z, c = me // 2, lax.rem(me, 2)
    other = 1 - c
    wide = HERE * HDIM
    right = {"sample": 2 * lax.rem(z + 1, chips) + c}
    left = {"sample": 2 * lax.rem(z + chips - 1, chips) + c}
    ways = (right, left)
    sibling = {"sample": 2 * z + other}
    unit = xs.shape[1]
    rows_all, features = res.shape
    sent = []

    def start(copy):
        copy.start()
        sent.append(copy)

    def fetch(src, dst, k):
        copy = pltpu.make_async_copy(src, dst, lsem.at[k])
        copy.start()
        return copy

    small = [
        fetch(a, b, 7 + i)
        for i, (a, b) in enumerate(
            ((q_in, qraw), (lens_in, lens), (res_in, res), (gain_in, gain), (ids_in, ids), (probs_in, probs))
        )
    ]
    fetch_g = fetch(gkv, gv, 1)
    fetch_kv = []
    for hp in range(2):
        for side in range(2):
            begin = (2 * side + hp) * HERE * HDIM
            fetch_kv.append(
                fetch(
                    kv.at[:, :, begin:begin + HERE * HDIM],
                    kvv.at[:, hp, :, side * HERE * HDIM:(side + 1) * HERE * HDIM],
                    13 + 2 * hp + side,
                )
            )

    barrier = pltpu.get_barrier_semaphore()

    def greet_sample(o, carry):
        pl.semaphore_signal(barrier, inc=1, device_id={"sample": lax.rem(me + o, n)}, device_id_type=MESH)
        return carry

    def greet_expert(o, carry):
        pl.semaphore_signal(barrier, inc=1, device_id={"expert": lax.rem(col + o, e)}, device_id_type=MESH)
        return carry

    lax.fori_loop(1, n, greet_sample, 0)
    lax.fori_loop(1, e, greet_expert, 0)

    for copy in small:
        copy.wait()
    for h in range(q.shape[1]):
        qwide[:, h, :] = qraw[:, h * HDIM:(h + 1) * HDIM].astype(F32)
    q[...] = qwide[...].astype(BF16)
    prompts = q.shape[0]
    gen = gv.shape[1]
    scale = HDIM ** (-0.5)
    for copy in fetch_kv:
        copy.wait()
    pl.semaphore_wait(barrier, n - 1 + e - 1)

    order = token_order(chips)
    where_of = {d: i for i, d in enumerate(order)}

    def q_pair(p, hp):
        return q.at[p, pl.ds(pl.multiple_of(hp * HERE * GROUPS, HERE * GROUPS), HERE * GROUPS)], rq.at[me]

    def m_pair(p, hp):
        return gmsg.at[p, hp], rm.at[me]

    def kv_pair(p, hp, slot):
        return kvv.at[p, hp], rkv.at[slot]

    def exchange(kind, dz, hp):
        p = lax.rem(z + dz, chips)
        slot = 2 * where_of[(chips - dz) % chips] + c
        src, dst = (q_pair(p, hp), m_pair(p, hp), kv_pair(p, hp, slot))[kind]
        target = {"sample": 2 * p + hp}
        start(remote(src, dst, ex_s.at[kind, 2 * dz + (hp if dz else 0)], ex_r.at[kind, slot], target))

    early = order[1:half]

    def send_all(kinds, distances):
        for dz in distances:
            for hp in range(2):
                for kind in kinds:
                    exchange(kind, dz, hp)

    send_all((2,), early)
    send_all((0,), order[1:])
    for kind in (0, 2):
        exchange(kind, 0, other)
    fetch_g.wait()
    tall = prompts * GROUPS
    of_row = lax.broadcasted_iota(jnp.int32, (tall, prompts), 0) // GROUPS
    is_row = of_row == lax.broadcasted_iota(jnp.int32, (tall, prompts), 1)
    length = jnp.sum(jnp.where(is_row, lens[...].astype(F32), 0.0), axis=1, keepdims=True)
    lane = lax.broadcasted_iota(jnp.int32, (tall, HDIM), 1)
    for hp in range(2):
        stats = jnp.zeros((tall, HDIM), F32)
        for hl in range(HERE):
            h = hp * HERE + hl
            query = q[:, h * GROUPS:(h + 1) * GROUPS, :].reshape(tall, HDIM)
            keys = gv[:, :, h * HDIM:(h + 1) * HDIM].reshape(prompts * gen, HDIM)
            vals = gv[:, :, (KVHEADS + h) * HDIM:(KVHEADS + h + 1) * HDIM].reshape(prompts * gen, HDIM)
            scores = lax.dot_general(query, keys, NT, preferred_element_type=F32) * scale
            row = lax.broadcasted_iota(jnp.int32, scores.shape, 0) // GROUPS
            at_key = (lax.broadcasted_iota(jnp.int32, scores.shape, 1) - row * gen).astype(F32)
            scores = jnp.where(jnp.logical_and(at_key >= 0.0, at_key < length), scores, NEGATIVE)
            highest = jnp.max(scores, axis=1, keepdims=True)
            weight = jnp.exp(scores - highest)
            total = jnp.sum(weight, axis=1, keepdims=True)
            got = jnp.dot(weight.astype(BF16), vals, preferred_element_type=F32) / total
            gmsg[:, hp, hl * GROUPS:(hl + 1) * GROUPS, :] = got.astype(BF16).reshape(prompts, GROUPS, HDIM)
            level = highest + jnp.log(total)
            for k in range(3):
                part = level.astype(BF16).astype(F32)
                level = level - part
                stats = jnp.where(lane == 3 * hl + k, part, stats)
        gmsg[:, hp, HERE * GROUPS:, :] = stats.astype(BF16).reshape(prompts, GROUPS, HDIM)
    exchange(1, 0, other)
    send_all((1,), order[1:])
    send_all((2,), order[half:])
    local = []
    for kind, (src, dst) in enumerate((q_pair(z, c), m_pair(z, c), kv_pair(z, c, c))):
        local.append(fetch(src, dst, kind))
    fetch_wo = fetch(wo, wov, 4)
    fetch_wg = fetch(wgu, wg, 5)
    fetch_wd = fetch(wdn, wd, 6)

    experts = place.shape[1]
    topk = ids.shape[1]
    named = jnp.zeros((topk, rows_all), F32)
    given = jnp.zeros((topk, rows_all), F32)
    for p in range(prompts):
        sample = lax.broadcasted_iota(jnp.int32, (n, rows_all), 0)
        there = lax.broadcasted_iota(jnp.int32, (n, rows_all), 1) == sample + p * n
        there = jnp.where(there, 1.0, 0.0).astype(BF16)
        named = named + jnp.dot(ids[p].astype(F32).astype(BF16), there, preferred_element_type=F32)
        rest = probs[p]
        for k in range(3):
            part = rest.astype(BF16)
            rest = rest - part.astype(F32)
            given = given + jnp.dot(part, there, preferred_element_type=F32)
    lane = lax.broadcasted_iota(jnp.int32, (rows_all, experts), 1)
    expert_row = lax.broadcasted_iota(jnp.int32, (experts, rows_all), 0).astype(F32)
    hits = jnp.zeros((experts, rows_all), F32)
    share_t = jnp.zeros((experts, rows_all), F32)
    for k in range(topk):
        same = expert_row == named[k:k + 1, :]
        hits = hits + jnp.where(same, 1.0, 0.0)
        share_t = share_t + jnp.where(same, given[k:k + 1, :], 0.0)
    square = (rows_all, rows_all)
    row_index = lax.broadcasted_iota(jnp.int32, square, 0)
    lane_index = lax.broadcasted_iota(jnp.int32, square, 1)
    above = jnp.where(row_index < lane_index, 1.0, 0.0).astype(BF16)
    eye_bf = jnp.where(row_index == lane_index, 1.0, 0.0).astype(BF16)
    before = jnp.dot(hits.astype(BF16), above, preferred_element_type=F32)
    place_t = jnp.where(hits > 0.5, before, -1.0).astype(BF16)
    place[...] = lax.dot_general(eye_bf, place_t, NT, preferred_element_type=F32).astype(BF16)
    at = lax.broadcasted_iota(jnp.int32, (e, unit, experts), 1)
    local_expert = jnp.zeros((e, unit, experts), jnp.int32)
    for j in range(1, EXP_COL):
        local_expert = local_expert + jnp.where(at >= CAP * j, 1, 0)
    slot_of = (at - CAP * local_expert).astype(F32)
    owner = lax.broadcasted_iota(jnp.int32, (e, unit, experts), 0) * EXP_COL + local_expert
    on_lane = lax.broadcasted_iota(jnp.int32, (e, unit, experts), 2)
    table = jnp.where(owner == on_lane, 1.0, 0.0).astype(BF16).reshape(e * unit, experts)
    seen = jnp.dot(table, place_t, preferred_element_type=F32)
    pick[...] = jnp.where(seen.reshape(e, unit, rows_all) == slot_of[:, :, :rows_all], 1.0, 0.0).astype(BF16)
    slot_table = jnp.where(on_lane == 0, slot_of, 0.0).astype(BF16).reshape(e * unit, experts)
    first_lane = jnp.where(lane == 0, 1.0, 0.0).astype(BF16)
    slot_row = lax.dot_general(first_lane, slot_table, NT, preferred_element_type=F32)
    placed = lax.dot_general(place[...], table, NT, preferred_element_type=F32)
    chosen = placed == slot_row
    for k, ref in enumerate((chi, clo)):
        part_t = share_t.astype(BF16)
        share_t = share_t - part_t.astype(F32)
        part = lax.dot_general(eye_bf, part_t, NT, preferred_element_type=F32).astype(BF16)
        spread_part = lax.dot_general(part, table, NT, preferred_element_type=F32)
        ref[...] = jnp.where(chosen, spread_part, 0.0).astype(BF16)

    for copy in local:
        copy.wait()

    def arrived(kind, slot):
        if kind == 0:
            src, dst = q_pair(0, 0)
        elif kind == 1:
            src, dst = m_pair(0, 0)
        else:
            src, dst = kv_pair(0, 0, slot)
        remote(src, dst, ex_s.at[kind, 1], ex_r.at[kind, slot], sibling).wait_recv()

    def arrive_all(kinds, low, high):
        def body(i, carry):
            for kind in kinds:
                arrived(kind, i)
            return carry

        lax.fori_loop(low, high, body, 0)

    for kind in range(3):
        arrived(kind, other)
    arrive_all((0, 1), 2, n)
    first = n // 2
    arrive_all((2,), 2, first)
    block = min(8, n)
    slab = block * GROUPS

    def absorb(h, i, low, high, highest, total, acc):
        own = pl.ds(i * block, block)
        query = rq[own, h * GROUPS:(h + 1) * GROUPS, :].reshape(slab, HDIM)
        lanes = slice(h * HDIM, (h + 1) * HDIM)
        count = (high - low) * rkv.shape[1]
        keys = rkv[low:high, :, lanes].reshape(count, HDIM)
        vals = rkv[low:high, :, wide + h * HDIM:wide + (h + 1) * HDIM].reshape(count, HDIM)
        scores = lax.dot_general(query, keys, NT, preferred_element_type=F32) * scale
        peak = jnp.maximum(highest, jnp.max(scores, axis=1, keepdims=True))
        kept = jnp.exp(highest - peak)
        weight = jnp.exp(scores - peak)
        total = total * kept + jnp.sum(weight, axis=1, keepdims=True)
        acc = acc * kept + jnp.dot(weight.astype(BF16), vals, preferred_element_type=F32)
        return peak, total, acc

    def slab_rows(i):
        return pl.ds(pl.multiple_of(i * slab, slab), slab)

    for h in range(HERE):

        def stage_one(i, carry, h=h):
            own = pl.ds(i * block, block)
            stats = rm[own, HERE * GROUPS:, :].reshape(slab, HDIM).astype(F32)
            level = stats[:, 3 * h:3 * h + 1] + stats[:, 3 * h + 1:3 * h + 2] + stats[:, 3 * h + 2:3 * h + 3]
            acc = rm[own, h * GROUPS:(h + 1) * GROUPS, :].reshape(slab, HDIM).astype(F32)
            peak, total, acc = absorb(h, i, 0, first, level, jnp.ones((slab, 1), F32), acc)
            mst[h, slab_rows(i), :] = jnp.broadcast_to(peak, (slab, HDIM))
            lst[h, slab_rows(i), :] = jnp.broadcast_to(total, (slab, HDIM))
            ost[h, slab_rows(i), :] = acc
            return carry

        lax.fori_loop(0, n // block, stage_one, 0)

    count = n * GROUPS
    r = lax.broadcasted_iota(jnp.int32, (count, count), 0)
    k = lax.broadcasted_iota(jnp.int32, (count, count), 1)
    swap = jnp.where(k == (lax.rem(r, n) * GROUPS + r // n), 1.0, 0.0).astype(BF16)
    at_rows = pl.ds(pl.multiple_of(z * n, n), n)
    width = HERE * GROUPS * HDIM
    cut = width // PIECES
    per_head = PIECES // HERE

    def part(core, b, u):
        return att.at[core, pl.ds(pl.multiple_of(b * n, n), n), u * cut:(u + 1) * cut]

    def goes(t, d, u):
        return t < half - 1 or (t == half - 1 and u % 2 == d)

    def ring_block(t, d):
        return lax.rem(z + (chips - 1 - t if d == 0 else 1 + t), chips)

    def along(t, d, u, b):
        ref = part(c, b, u)
        return remote(ref, ref, ag_s.at[d, t, u], ag_r.at[d, t, u], ways[d])

    def across(core, t, d, u, b):
        ref = part(core, b, u)
        return remote(ref, ref, sib_s.at[d, t, u], sib_r.at[d, t, u], sibling)

    def own_across(core, u):
        ref = part(core, z, u)
        return remote(ref, ref, own_sem.at[0, u], own_sem.at[1, u], sibling)

    arrive_all((2,), first, n)
    for h in range(HERE):

        def stage_two(i, carry, h=h):
            peak = mst[h, slab_rows(i), 0:1]
            total = lst[h, slab_rows(i), 0:1]
            peak, total, acc = absorb(h, i, first, n, peak, total, ost[h, slab_rows(i), :])
            obuf[h, slab_rows(i), :] = (acc / total).astype(BF16)
            return carry

        lax.fori_loop(0, n // block, stage_two, 0)
        swapped = jnp.dot(swap, obuf[h], preferred_element_type=F32).astype(BF16)
        for g in range(GROUPS):
            begin = (h * GROUPS + g) * HDIM
            att[c, at_rows, begin:begin + HDIM] = swapped[g * n:(g + 1) * n, :]
        for u in range(h * per_head, (h + 1) * per_head):
            for d in range(2):
                if goes(0, d, u):
                    start(along(0, d, u, z))
        for u in range(h * per_head, (h + 1) * per_head):
            start(own_across(c, u))

    fetch_wo.wait()
    projected = jnp.zeros((rows_all, features), F32)

    def project(acc, core, u):
        lanes = slice(u * cut, (u + 1) * cut)
        return acc + jnp.dot(att[core, :, lanes], wov[core, lanes, :], preferred_element_type=F32)

    for t in range(half):
        for u in range(PIECES):
            for d in range(2):
                if not goes(t, d, u):
                    continue
                b = ring_block(t, d)
                along(t, d, u, b).wait_recv()
                if goes(t + 1, d, u):
                    start(along(t + 1, d, u, b))
                start(across(c, t, d, u, b))
            if t == half - 1:
                projected = project(projected, c, u)
    for u in range(PIECES):
        own_across(other, u).wait_recv()
        for t in range(half):
            for d in range(2):
                if goes(t, d, u):
                    across(other, t, d, u, ring_block(t, d)).wait_recv()
        projected = project(projected, other, u)

    mixed[...] = projected.astype(BF16)
    stream = res[...].astype(F32) + projected
    y[...] = (stream * gain[...]).astype(BF16)
    shift = each * (col // each)

    def target_of(k, i):
        return each * lax.rem(col // each + chips + chips - k, chips) + i

    def slot_at(k):
        return k * each + lax.rem(col, each)

    def send_rows(k):
        for i in range(each):
            to = target_of(k, i)
            xs[to] = jnp.dot(pick[to], y[...], preferred_element_type=F32).astype(BF16)

            @pl.when(to != col)
            def _(k=k, to=to):
                remote(xs.at[to], xr.at[slot_at(k)], x_s.at[to], x_r.at[slot_at(k)], {"expert": to}).start()

            @pl.when(to == col)
            def _(k=k, to=to):
                xr[slot_at(k)] = xs[to]

    send_rows(ring_block(0, 0))
    send_rows(ring_block(0, 1))

    def wait_rows(k):
        for i in range(each):
            b = k * each + i
            src = lax.rem(b + shift, e)

            @pl.when(src != col)
            def _(b=b, src=src):
                remote(xs.at[0], xr.at[b], x_s.at[0], x_r.at[b], {"expert": src}).wait_recv()

    eye = lax.broadcasted_iota(jnp.int32, square, 0) == lax.broadcasted_iota(jnp.int32, square, 1)
    column = jnp.sum(stream * stream, axis=1, keepdims=True)
    flat = jnp.sum(jnp.where(eye, column, 0.0), axis=0, keepdims=True)
    sqs[...] = jnp.broadcast_to(flat, sqs.shape)
    for o in range(1, n):
        start(remote(sqs, sqr.at[o], sq_ss.at[o], sq_rs.at[o], {"sample": lax.rem(me + o, n)}))

    quarter = pown.shape[4]
    ff = 4 * quarter
    fetch_wg.wait()

    def chunk(d, t):
        return lax.rem(z + (chips + chips - 1 - t if d == 0 else 1 + t), chips)

    def partial(gq, dst, d, k):
        own = pl.ds(k * each, each)
        for side in range(2):
            lanes = pl.ds(pl.multiple_of(side * ff + gq * quarter, 128), quarter)
            tiles = {}
            for j, (low, high) in enumerate(spans()):
                lhs = xr[own, low:high, :].reshape(each * (high - low), features)
                got = jnp.dot(lhs, wg[j, :, lanes], preferred_element_type=F32)
                got = got.reshape(each, high - low, quarter)
                for tile in range(low // TILE, high // TILE):
                    piece = got[:, tile * TILE - low:(tile + 1) * TILE - low, :]
                    tiles.setdefault(tile, []).append((j, piece))
            for tile, parts in tiles.items():
                dst[d, own, side, tile * TILE:(tile + 1) * TILE, :] = merge_tile(tile, parts).astype(BF16)

    def pair(d, t):
        own = pl.ds(chunk(d, t) * each, each)
        return remote(psib.at[d, own], rsib.at[d, own], ps_s.at[d, t], ps_r.at[d, t], sibling)

    def hop(d, t, u, w):
        b = chunk(d, t) * each + u
        return remote(pown.at[d, b, w], rr.at[d, t, u, w], rs_s.at[d, t, u, w], rs_r.at[d, t, u, w], ways[d])

    def pair_sum(d, b, w):
        return pown[d, b, w].astype(F32) + rsib[d, b, w].astype(F32)

    def prepare(t):
        for d in range(2):
            partial(2 * other + d, psib, d, chunk(d, t))
            pair(d, t).start()
        for d in range(2):
            partial(2 * c + d, pown, d, chunk(d, t))

    def norm_factor():
        squares = sqs[...]
        for o in range(1, n):
            remote(
                sqs, sqr.at[o], sq_ss.at[o], sq_rs.at[o], {"sample": lax.rem(me + n - o, n)}
            ).wait_recv()
            squares = squares + sqr[o]
        factor = lax.rsqrt(squares / (features * n) + EPSILON)[0:1, :]
        for i in range(each):
            to = target_of(z, i)
            values = jnp.sum(pick[to].astype(F32) * factor, axis=1, keepdims=True)
            fsend[i] = jnp.broadcast_to(values, fsend.shape[1:])

            @pl.when(to != col)
            def _(i=i, to=to):
                place_at = lax.rem(col, each)
                remote(fsend.at[i], frecv.at[place_at], f_s.at[i], f_r.at[place_at], {"expert": to}).start()

            @pl.when(to == col)
            def _(i=i):
                frecv[lax.rem(col, each)] = fsend[i]

    def ring(t, carry):
        @pl.when(t < half)
        def _():
            wait_rows(chunk(0, t))

        @pl.when(t < half - 1)
        def _():
            wait_rows(chunk(1, t))
            send_rows(chunk(0, t + 1))

        @pl.when(t < half - 2)
        def _():
            send_rows(chunk(1, t + 1))

        @pl.when(t == half)
        def _():
            send_rows(z)

        prepare(t)
        for d in range(2):
            pair(d, t).wait_recv()
        for u in range(each):
            for w in range(2):
                for d in range(2):
                    b = chunk(d, t) * each + u

                    @pl.when(t == 0)
                    def _(d=d, b=b, w=w):
                        pown[d, b, w] = pair_sum(d, b, w).astype(BF16)

                    @pl.when(t > 0)
                    def _(d=d, b=b, u=u, w=w):
                        hop(d, t - 1, u, w).wait_recv()
                        value = pair_sum(d, b, w) + rr[d, t - 1, u, w].astype(F32)
                        pown[d, b, w] = value.astype(BF16)

                    hop(d, t, u, w).start()

        @pl.when(t == 1)
        def _():
            norm_factor()

        return carry

    lax.fori_loop(0, chips - 1, ring, 0)
    wait_rows(z)
    prepare(chips - 1)
    for i in range(each):
        src = lax.rem(z * each + i + shift, e)

        @pl.when(src != col)
        def _(i=i, src=src):
            remote(fsend.at[0], frecv.at[i], f_s.at[0], f_r.at[i], {"expert": src}).wait_recv()

    for d in range(2):
        pair(d, chips - 1).wait_recv()

    def act_part(core, b, w):
        return act.at[core, b, w]

    def spread(d, t, u, w, b):
        ref = act_part(c, b, w)
        return remote(ref, ref, aa_s.at[d, t, u, w], aa_r.at[d, t, u, w], ways[d])

    def hand(core, d, t, u, w, b):
        ref = act_part(core, b, w)
        return remote(ref, ref, fw_s.at[d, t, u, w], fw_r.at[d, t, u, w], sibling)

    def own_hand(core, u, w):
        ref = act_part(core, z * each + u, w)
        return remote(ref, ref, me_sem.at[0, u, w], me_sem.at[1, u, w], sibling)

    for u in range(each):
        b = z * each + u
        factor = frecv[u][:, 0:1]
        for part_of in range(2):
            sums = []
            for w in range(2):
                hop(part_of, chips - 2, u, w).wait_recv()
                value = pair_sum(part_of, b, w) + rr[part_of, chips - 2, u, w].astype(F32)
                sums.append(value * factor)
            gate, up = sums
            act[c, b, part_of] = (gate / (1.0 + jnp.exp(-gate)) * up).astype(BF16)
            for d in range(2):
                if goes(0, d, u):
                    start(spread(d, 0, u, part_of, b))
            start(own_hand(c, u, part_of))
    fetch_wd.wait()

    def finish(slots):
        tiles = {}
        count = len(slots)
        for j, (low, high) in enumerate(spans()):
            got = None
            for core in range(2):
                halves = [
                    jnp.concatenate([act[core, b, w, low:high, :] for b in slots], axis=0) for w in range(2)
                ]
                lhs = jnp.concatenate(halves, axis=1)
                depth = slice(core * 2 * quarter, (core + 1) * 2 * quarter)
                term = jnp.dot(lhs, wd[j, depth, :], preferred_element_type=F32)
                got = term if got is None else got + term
            got = got.reshape(count, high - low, got.shape[1])
            for tile in range(low // TILE, high // TILE):
                piece = got[:, tile * TILE - low:(tile + 1) * TILE - low, :]
                tiles.setdefault(tile, []).append((j, piece))
        done = {tile: merge_tile(tile, parts).astype(BF16) for tile, parts in tiles.items()}
        for i, b in enumerate(slots):
            for tile, value in done.items():
                osend[b, tile * TILE:(tile + 1) * TILE, :] = value[i]
            target = lax.rem(b + shift, e)

            @pl.when(target != col)
            def _(b=b, target=target):
                remote(osend.at[b], oret.at[col], o_s.at[b], o_r.at[col], {"expert": target}).start()

            @pl.when(target == col)
            def _(b=b):
                oret[col] = osend[b]

    def complete(pending):
        for b, copies in pending:
            for copy in copies:
                copy.wait_recv()
        finish([b for b, copies in pending])

    pending = [(z * each + u, [own_hand(other, u, w) for w in range(2)]) for u in range(each)]
    for t in range(half):
        if t == half - 1:
            complete(pending)
            pending = []
        fresh = []
        for u in range(each):
            for d in range(2):
                if not goes(t, d, u):
                    continue
                fresh.append(
                    (ring_block(t, d) * each + u, [hand(other, d, t, u, w, ring_block(t, d) * each + u) for w in range(2)])
                )
            for w in range(2):
                for d in range(2):
                    if not goes(t, d, u):
                        continue
                    b = ring_block(t, d) * each + u
                    spread(d, t, u, w, b).wait_recv()
                    if goes(t + 1, d, u):
                        start(spread(d, t + 1, u, w, b))
                    start(hand(c, d, t, u, w, b))
        if pending:
            complete(pending)
        pending = fresh
    complete(pending)

    def wait_return(o, carry):
        src = lax.rem(col + o, e)
        remote(osend.at[0], oret.at[src], o_s.at[0], o_r.at[src], {"expert": src}).wait_recv()
        return carry

    lax.fori_loop(1, e, wait_return, 0)
    returned = oret[...].reshape(e * unit, out.shape[1])
    total = jnp.dot(chi[...], returned, preferred_element_type=F32)
    total = total + jnp.dot(clo[...], returned, preferred_element_type=F32)
    out[...] = total.astype(BF16)

    for copy in sent:
        copy.wait_send()

    def drain(t, carry):
        for d in range(2):
            pair(d, t).wait_send()

            @pl.when(t < chips - 1)
            def _(d=d):
                for u in range(each):
                    for w in range(2):
                        hop(d, t, u, w).wait_send()

        return carry

    lax.fori_loop(0, chips, drain, 0)

    def drain_out(b, carry):
        target = lax.rem(b + shift, e)

        @pl.when(target != col)
        def _():
            remote(osend.at[b], oret.at[col], o_s.at[b], o_r.at[col], {"expert": target}).wait_send()

        @pl.when(b != col)
        def _():
            remote(xs.at[b], xr.at[0], x_s.at[b], x_r.at[0], {"expert": b}).wait_send()

        return carry

    lax.fori_loop(0, e, drain_out, 0)
    for i in range(each):
        to = target_of(z, i)

        @pl.when(to != col)
        def _(i=i, to=to):
            remote(fsend.at[i], frecv.at[0], f_s.at[i], f_r.at[0], {"expert": to}).wait_send()


def on_device(
    n, e, queries, prompt_kv, gen_kv, gen_lengths, out_proj, residual, norm_gain,
    w_gate_up, w_down, routes, route_probs,
):
    prompts = queries.shape[0]
    rows = prompts * n
    features = residual.shape[2]
    out_features = w_down.shape[2]
    chips = n // 2
    half = chips // 2
    each = e // chips
    unit = -(-EXP_COL * CAP // TILE) * TILE
    heads = queries.shape[2] // HDIM
    topk = routes.shape[2]
    width = HERE * GROUPS * HDIM
    wide = HERE * HDIM
    tokens, gen = prompt_kv.shape[1], gen_kv.shape[2]
    quarter = w_gate_up.shape[2] // 8
    table = 128
    hbm = pl.BlockSpec(memory_space=pltpu.HBM)
    vmem = pl.BlockSpec(memory_space=pltpu.VMEM)
    dma = pltpu.SemaphoreType.DMA
    buf = pltpu.VMEM
    mixed, expert_out = pl.pallas_call(
        functools.partial(kernel, n, e),
        out_shape=(
            pltpu.VMEM((rows, features), BF16),
            pltpu.VMEM((rows, out_features), BF16),
        ),
        in_specs=[hbm] * 11,
        out_specs=(vmem, vmem),
        scratch_shapes=[
            buf((prompts, heads * HDIM), BF16),
            buf((prompts, heads, HDIM), F32),
            buf((prompts, heads, HDIM), BF16),
            buf((1, prompts), jnp.int32),
            buf((rows, features), BF16),
            buf((1, features), F32),
            buf((prompts, topk, n), jnp.int32),
            buf((prompts, topk, n), F32),
            buf((prompts, 2, tokens, 2 * wide), BF16),
            buf((prompts, gen, gen_kv.shape[3]), BF16),
            buf((prompts, 2, (HERE + 1) * GROUPS, HDIM), BF16),
            buf((n, HERE * GROUPS, HDIM), BF16),
            buf((n, (HERE + 1) * GROUPS, HDIM), BF16),
            buf((n, tokens, 2 * wide), BF16),
            buf((2, width, features), BF16),
            buf(w_gate_up.shape, BF16),
            buf(w_down.shape, BF16),
            buf((HERE, n * GROUPS, HDIM), F32),
            buf((HERE, n * GROUPS, HDIM), F32),
            buf((HERE, n * GROUPS, HDIM), F32),
            buf((HERE, n * GROUPS, HDIM), BF16),
            buf((2, rows, width), BF16),
            buf((8, rows), F32),
            buf((n, 8, rows), F32),
            buf((rows, table), BF16),
            buf((e, unit, rows), BF16),
            buf((rows, e * unit), BF16),
            buf((rows, e * unit), BF16),
            buf((rows, features), BF16),
            buf((e, unit, features), BF16),
            buf((e, unit, features), BF16),
            buf((2, e, 2, unit, quarter), BF16),
            buf((2, e, 2, unit, quarter), BF16),
            buf((2, e, 2, unit, quarter), BF16),
            buf((2, chips - 1, each, 2, unit, quarter), BF16),
            buf((2, e, 2, unit, quarter), BF16),
            buf((e, unit, out_features), BF16),
            buf((e, unit, out_features), BF16),
            buf((each, unit, HDIM), F32),
            buf((each, unit, HDIM), F32),
            dma((17,)),
            dma((3, n)),
            dma((3, n)),
            dma((2, half, PIECES)),
            dma((2, half, PIECES)),
            dma((2, half, PIECES)),
            dma((2, half, PIECES)),
            dma((2, PIECES)),
            dma((n,)),
            dma((n,)),
            dma((e,)),
            dma((e,)),
            dma((2, chips)),
            dma((2, chips)),
            dma((2, chips - 1, each, 2)),
            dma((2, chips - 1, each, 2)),
            dma((2, half, each, 2)),
            dma((2, half, each, 2)),
            dma((2, half, each, 2)),
            dma((2, half, each, 2)),
            dma((2, each, 2)),
            dma((e,)),
            dma((e,)),
            dma((each,)),
            dma((each,)),
        ],
        compiler_params=pltpu.CompilerParams(
            collective_id=0, has_side_effects=True, vmem_limit_bytes=56 << 20
        ),
        name="decode_step",
    )(
        queries.reshape(prompts, heads * HDIM),
        gen_lengths.T,
        prompt_kv,
        gen_kv.reshape(prompts, gen, gen_kv.shape[3]),
        out_proj.reshape(2, width, features),
        residual.reshape(rows, features),
        norm_gain.reshape(1, features),
        jnp.swapaxes(routes, 1, 2),
        jnp.swapaxes(route_probs, 1, 2),
        w_gate_up,
        w_down,
    )
    shape = (prompts, n, features)
    return (mixed.reshape(shape), expert_out.reshape(shape))


def solution(mesh):
    placed = (
        P("expert", "sample", None),
        P("expert", "sample", None),
        P("expert", "sample", None, None),
        P("expert", "sample"),
        P(None, "sample"),
        P("expert", None, "sample"),
        P("sample"),
        P("expert", "sample", None),
        P("expert", None, "sample"),
        P("expert", None, None),
        P("expert", None, None),
    )
    return jax.shard_map(
        functools.partial(on_device, mesh.shape["sample"], mesh.shape["expert"]),
        mesh=mesh,
        in_specs=placed,
        out_specs=(P("expert", None, "sample"), P("expert", None, "sample")),
        check_vma=False,
    )
```

```python
import functools

import jax
import jax.numpy as jnp
from jax import lax
from jax.experimental import pallas as pl
from jax.experimental.pallas import tpu as pltpu
from jax.sharding import PartitionSpec as P

MESH = pl.DeviceIdType.MESH
HDIM = 128
GROUPS = 16
KVHEADS = 4
HERE = 2
EXP_COL = 3
CAP = 26
TILE = 16
PIECES = 4
NEGATIVE = -1e30
EPSILON = 1e-06
F32 = jnp.float32
BF16 = jnp.bfloat16
NT = (((1,), (1,)), ((), ()))


def remote(src, dst, send, recv, device):
    return pltpu.make_async_remote_copy(
        src_ref=src, dst_ref=dst, send_sem=send, recv_sem=recv, device_id=device, device_id_type=MESH
    )


def spans():
    out = []
    for j in range(EXP_COL):
        low = CAP * j // TILE * TILE
        high = -(-CAP * (j + 1) // TILE) * TILE
        out.append((low, high))
    return out


def merge_tile(tile, parts):
    if len(parts) == 1:
        return parts[0][1]
    (first, a), (second, b) = parts
    shape = (1,) * (a.ndim - 2) + (TILE, 1)
    rows = lax.broadcasted_iota(jnp.int32, shape, a.ndim - 2) + tile * TILE
    return jnp.where(rows < CAP * (first + 1), a, b)


def token_order(chips):
    return [0] + sorted(range(1, chips), key=lambda d: -min(d, chips - d))


def kernel(
    n, e,
    q_in, lens_in, kv, gkv, wo, res_in, gain_in, ids_in, probs_in, wgu, wdn,
    mixed, out,
    qraw, qwide, q, lens, res, gain, ids, probs, kvv, gv, gmsg, rq, rm, rkv, wov, wg, wd, ost, mst, lst, obuf, att, sqs, sqr,
    place, pick, chi, clo, y, xs, xr, pown, psib, rsib, rr, act, osend, oret, fsend, frecv,
    lsem, ex_s, ex_r, ag_s, ag_r, sib_s, sib_r, own_sem, sq_ss, sq_rs,
    x_s, x_r, ps_s, ps_r, rs_s, rs_r, aa_s, aa_r, fw_s, fw_r, me_sem, o_s, o_r, f_s, f_r,
):
    chips = n // 2
    half = chips // 2
    each = e // chips
    me = lax.axis_index("sample")
    col = lax.axis_index("expert")
    z, c = me // 2, lax.rem(me, 2)
    other = 1 - c
    wide = HERE * HDIM
    right = {"sample": 2 * lax.rem(z + 1, chips) + c}
    left = {"sample": 2 * lax.rem(z + chips - 1, chips) + c}
    ways = (right, left)
    sibling = {"sample": 2 * z + other}
    unit = xs.shape[1]
    rows_all, features = res.shape
    sent = []

    def start(copy):
        copy.start()
        sent.append(copy)

    def fetch(src, dst, k):
        copy = pltpu.make_async_copy(src, dst, lsem.at[k])
        copy.start()
        return copy

    small = [
        fetch(a, b, 7 + i)
        for i, (a, b) in enumerate(
            ((q_in, qraw), (lens_in, lens), (res_in, res), (gain_in, gain), (ids_in, ids), (probs_in, probs))
        )
    ]
    fetch_g = fetch(gkv, gv, 1)
    fetch_kv = []
    for hp in range(2):
        for side in range(2):
            begin = (2 * side + hp) * HERE * HDIM
            fetch_kv.append(
                fetch(
                    kv.at[:, :, begin:begin + HERE * HDIM],
                    kvv.at[:, hp, :, side * HERE * HDIM:(side + 1) * HERE * HDIM],
                    13 + 2 * hp + side,
                )
            )

    barrier = pltpu.get_barrier_semaphore()

    def greet_sample(o, carry):
        pl.semaphore_signal(barrier, inc=1, device_id={"sample": lax.rem(me + o, n)}, device_id_type=MESH)
        return carry

    def greet_expert(o, carry):
        pl.semaphore_signal(barrier, inc=1, device_id={"expert": lax.rem(col + o, e)}, device_id_type=MESH)
        return carry

    lax.fori_loop(1, n, greet_sample, 0)
    lax.fori_loop(1, e, greet_expert, 0)

    for copy in small:
        copy.wait()
    for h in range(q.shape[1]):
        qwide[:, h, :] = qraw[:, h * HDIM:(h + 1) * HDIM].astype(F32)
    q[...] = qwide[...].astype(BF16)
    prompts = q.shape[0]
    gen = gv.shape[1]
    scale = HDIM ** (-0.5)
    for copy in fetch_kv:
        copy.wait()
    pl.semaphore_wait(barrier, n - 1 + e - 1)

    order = token_order(chips)
    where_of = {d: i for i, d in enumerate(order)}

    def q_pair(p, hp):
        return q.at[p, pl.ds(pl.multiple_of(hp * HERE * GROUPS, HERE * GROUPS), HERE * GROUPS)], rq.at[me]

    def m_pair(p, hp):
        return gmsg.at[p, hp], rm.at[me]

    def kv_pair(p, hp, slot):
        return kvv.at[p, hp], rkv.at[slot]

    def exchange(kind, dz, hp):
        p = lax.rem(z + dz, chips)
        slot = 2 * where_of[(chips - dz) % chips] + c
        src, dst = (q_pair(p, hp), m_pair(p, hp), kv_pair(p, hp, slot))[kind]
        target = {"sample": 2 * p + hp}
        start(remote(src, dst, ex_s.at[kind, 2 * dz + (hp if dz else 0)], ex_r.at[kind, slot], target))

    early = order[1:half]

    def send_all(kinds, distances):
        for dz in distances:
            for hp in range(2):
                for kind in kinds:
                    exchange(kind, dz, hp)

    send_all((2,), early)
    send_all((0,), order[1:])
    for kind in (0, 2):
        exchange(kind, 0, other)
    fetch_g.wait()
    tall = prompts * GROUPS
    of_row = lax.broadcasted_iota(jnp.int32, (tall, prompts), 0) // GROUPS
    is_row = of_row == lax.broadcasted_iota(jnp.int32, (tall, prompts), 1)
    length = jnp.sum(jnp.where(is_row, lens[...].astype(F32), 0.0), axis=1, keepdims=True)
    lane = lax.broadcasted_iota(jnp.int32, (tall, HDIM), 1)
    for hp in range(2):
        stats = jnp.zeros((tall, HDIM), F32)
        for hl in range(HERE):
            h = hp * HERE + hl
            query = q[:, h * GROUPS:(h + 1) * GROUPS, :].reshape(tall, HDIM)
            keys = gv[:, :, h * HDIM:(h + 1) * HDIM].reshape(prompts * gen, HDIM)
            vals = gv[:, :, (KVHEADS + h) * HDIM:(KVHEADS + h + 1) * HDIM].reshape(prompts * gen, HDIM)
            scores = lax.dot_general(query, keys, NT, preferred_element_type=F32) * scale
            row = lax.broadcasted_iota(jnp.int32, scores.shape, 0) // GROUPS
            at_key = (lax.broadcasted_iota(jnp.int32, scores.shape, 1) - row * gen).astype(F32)
            scores = jnp.where(jnp.logical_and(at_key >= 0.0, at_key < length), scores, NEGATIVE)
            highest = jnp.max(scores, axis=1, keepdims=True)
            weight = jnp.exp(scores - highest)
            total = jnp.sum(weight, axis=1, keepdims=True)
            got = jnp.dot(weight.astype(BF16), vals, preferred_element_type=F32) / total
            gmsg[:, hp, hl * GROUPS:(hl + 1) * GROUPS, :] = got.astype(BF16).reshape(prompts, GROUPS, HDIM)
            level = highest + jnp.log(total)
            for k in range(3):
                part = level.astype(BF16).astype(F32)
                level = level - part
                stats = jnp.where(lane == 3 * hl + k, part, stats)
        gmsg[:, hp, HERE * GROUPS:, :] = stats.astype(BF16).reshape(prompts, GROUPS, HDIM)
    exchange(1, 0, other)
    send_all((1,), order[1:])
    send_all((2,), order[half:])
    local = []
    for kind, (src, dst) in enumerate((q_pair(z, c), m_pair(z, c), kv_pair(z, c, c))):
        local.append(fetch(src, dst, kind))
    fetch_wo = fetch(wo, wov, 4)
    fetch_wg = fetch(wgu, wg, 5)
    fetch_wd = fetch(wdn, wd, 6)

    experts = place.shape[1]
    topk = ids.shape[1]
    named = jnp.zeros((topk, rows_all), F32)
    given = jnp.zeros((topk, rows_all), F32)
    for p in range(prompts):
        sample = lax.broadcasted_iota(jnp.int32, (n, rows_all), 0)
        there = lax.broadcasted_iota(jnp.int32, (n, rows_all), 1) == sample + p * n
        there = jnp.where(there, 1.0, 0.0).astype(BF16)
        named = named + jnp.dot(ids[p].astype(F32).astype(BF16), there, preferred_element_type=F32)
        rest = probs[p]
        for k in range(3):
            part = rest.astype(BF16)
            rest = rest - part.astype(F32)
            given = given + jnp.dot(part, there, preferred_element_type=F32)
    lane = lax.broadcasted_iota(jnp.int32, (rows_all, experts), 1)
    expert_row = lax.broadcasted_iota(jnp.int32, (experts, rows_all), 0).astype(F32)
    hits = jnp.zeros((experts, rows_all), F32)
    share_t = jnp.zeros((experts, rows_all), F32)
    for k in range(topk):
        same = expert_row == named[k:k + 1, :]
        hits = hits + jnp.where(same, 1.0, 0.0)
        share_t = share_t + jnp.where(same, given[k:k + 1, :], 0.0)
    square = (rows_all, rows_all)
    row_index = lax.broadcasted_iota(jnp.int32, square, 0)
    lane_index = lax.broadcasted_iota(jnp.int32, square, 1)
    above = jnp.where(row_index < lane_index, 1.0, 0.0).astype(BF16)
    eye_bf = jnp.where(row_index == lane_index, 1.0, 0.0).astype(BF16)
    before = jnp.dot(hits.astype(BF16), above, preferred_element_type=F32)
    place_t = jnp.where(hits > 0.5, before, -1.0).astype(BF16)
    place[...] = lax.dot_general(eye_bf, place_t, NT, preferred_element_type=F32).astype(BF16)
    at = lax.broadcasted_iota(jnp.int32, (e, unit, experts), 1)
    local_expert = jnp.zeros((e, unit, experts), jnp.int32)
    for j in range(1, EXP_COL):
        local_expert = local_expert + jnp.where(at >= CAP * j, 1, 0)
    slot_of = (at - CAP * local_expert).astype(F32)
    owner = lax.broadcasted_iota(jnp.int32, (e, unit, experts), 0) * EXP_COL + local_expert
    on_lane = lax.broadcasted_iota(jnp.int32, (e, unit, experts), 2)
    table = jnp.where(owner == on_lane, 1.0, 0.0).astype(BF16).reshape(e * unit, experts)
    seen = jnp.dot(table, place_t, preferred_element_type=F32)
    pick[...] = jnp.where(seen.reshape(e, unit, rows_all) == slot_of[:, :, :rows_all], 1.0, 0.0).astype(BF16)
    slot_table = jnp.where(on_lane == 0, slot_of, 0.0).astype(BF16).reshape(e * unit, experts)
    first_lane = jnp.where(lane == 0, 1.0, 0.0).astype(BF16)
    share_parts = []
    for k in range(2):
        part_t = share_t.astype(BF16)
        share_t = share_t - part_t.astype(F32)
        share_parts.append(lax.dot_general(eye_bf, part_t, NT, preferred_element_type=F32).astype(BF16))
    for p in range(chips):
        band = slice(p * each * unit, (p + 1) * each * unit)
        slot_row = lax.dot_general(first_lane, slot_table[band], NT, preferred_element_type=F32)
        placed = lax.dot_general(place[...], table[band], NT, preferred_element_type=F32)
        chosen = placed == slot_row
        for ref, part in zip((chi, clo), share_parts):
            spread_part = lax.dot_general(part, table[band], NT, preferred_element_type=F32)
            ref[p] = jnp.where(chosen, spread_part, 0.0).astype(BF16)

    for copy in local:
        copy.wait()

    def arrived(kind, slot):
        if kind == 0:
            src, dst = q_pair(0, 0)
        elif kind == 1:
            src, dst = m_pair(0, 0)
        else:
            src, dst = kv_pair(0, 0, slot)
        remote(src, dst, ex_s.at[kind, 1], ex_r.at[kind, slot], sibling).wait_recv()

    def arrive_all(kinds, low, high):
        def body(i, carry):
            for kind in kinds:
                arrived(kind, i)
            return carry

        lax.fori_loop(low, high, body, 0)

    for kind in range(3):
        arrived(kind, other)
    arrive_all((0, 1), 2, n)
    first = n // 2
    arrive_all((2,), 2, first)
    block = min(8, n)
    slab = block * GROUPS

    def absorb(h, i, low, high, highest, total, acc):
        own = pl.ds(i * block, block)
        query = rq[own, h * GROUPS:(h + 1) * GROUPS, :].reshape(slab, HDIM)
        lanes = slice(h * HDIM, (h + 1) * HDIM)
        count = (high - low) * rkv.shape[1]
        keys = rkv[low:high, :, lanes].reshape(count, HDIM)
        vals = rkv[low:high, :, wide + h * HDIM:wide + (h + 1) * HDIM].reshape(count, HDIM)
        scores = lax.dot_general(query, keys, NT, preferred_element_type=F32) * scale
        peak = jnp.maximum(highest, jnp.max(scores, axis=1, keepdims=True))
        kept = jnp.exp(highest - peak)
        weight = jnp.exp(scores - peak)
        total = total * kept + jnp.sum(weight, axis=1, keepdims=True)
        acc = acc * kept + jnp.dot(weight.astype(BF16), vals, preferred_element_type=F32)
        return peak, total, acc

    def slab_rows(i):
        return pl.ds(pl.multiple_of(i * slab, slab), slab)

    for h in range(HERE):

        def stage_one(i, carry, h=h):
            own = pl.ds(i * block, block)
            stats = rm[own, HERE * GROUPS:, :].reshape(slab, HDIM).astype(F32)
            level = stats[:, 3 * h:3 * h + 1] + stats[:, 3 * h + 1:3 * h + 2] + stats[:, 3 * h + 2:3 * h + 3]
            acc = rm[own, h * GROUPS:(h + 1) * GROUPS, :].reshape(slab, HDIM).astype(F32)
            peak, total, acc = absorb(h, i, 0, first, level, jnp.ones((slab, 1), F32), acc)
            mst[h, slab_rows(i), :] = jnp.broadcast_to(peak, (slab, HDIM))
            lst[h, slab_rows(i), :] = jnp.broadcast_to(total, (slab, HDIM))
            ost[h, slab_rows(i), :] = acc
            return carry

        lax.fori_loop(0, n // block, stage_one, 0)

    count = n * GROUPS
    r = lax.broadcasted_iota(jnp.int32, (count, count), 0)
    k = lax.broadcasted_iota(jnp.int32, (count, count), 1)
    swap = jnp.where(k == (lax.rem(r, n) * GROUPS + r // n), 1.0, 0.0).astype(BF16)
    at_rows = pl.ds(pl.multiple_of(z * n, n), n)
    width = HERE * GROUPS * HDIM
    cut = width // PIECES
    per_head = PIECES // HERE

    def part(core, b, u):
        return att.at[core, pl.ds(pl.multiple_of(b * n, n), n), u * cut:(u + 1) * cut]

    def goes(t, d, u):
        return t < half - 1 or (t == half - 1 and u % 2 == d)

    def ring_block(t, d):
        return lax.rem(z + (chips - 1 - t if d == 0 else 1 + t), chips)

    def along(t, d, u, b):
        ref = part(c, b, u)
        return remote(ref, ref, ag_s.at[d, t, u], ag_r.at[d, t, u], ways[d])

    def across(core, t, d, u, b):
        ref = part(core, b, u)
        return remote(ref, ref, sib_s.at[d, t, u], sib_r.at[d, t, u], sibling)

    def own_across(core, u):
        ref = part(core, z, u)
        return remote(ref, ref, own_sem.at[0, u], own_sem.at[1, u], sibling)

    arrive_all((2,), first, n)
    for h in range(HERE):

        def stage_two(i, carry, h=h):
            peak = mst[h, slab_rows(i), 0:1]
            total = lst[h, slab_rows(i), 0:1]
            peak, total, acc = absorb(h, i, first, n, peak, total, ost[h, slab_rows(i), :])
            obuf[h, slab_rows(i), :] = (acc / total).astype(BF16)
            return carry

        lax.fori_loop(0, n // block, stage_two, 0)
        swapped = jnp.dot(swap, obuf[h], preferred_element_type=F32).astype(BF16)
        for g in range(GROUPS):
            begin = (h * GROUPS + g) * HDIM
            att[c, at_rows, begin:begin + HDIM] = swapped[g * n:(g + 1) * n, :]
        for u in range(h * per_head, (h + 1) * per_head):
            for d in range(2):
                if goes(0, d, u):
                    start(along(0, d, u, z))
        for u in range(h * per_head, (h + 1) * per_head):
            start(own_across(c, u))

    fetch_wo.wait()
    projected = jnp.zeros((rows_all, features), F32)

    def project(acc, core, u):
        lanes = slice(u * cut, (u + 1) * cut)
        return acc + jnp.dot(att[core, :, lanes], wov[core, lanes, :], preferred_element_type=F32)

    for t in range(half):
        for u in range(PIECES):
            for d in range(2):
                if not goes(t, d, u):
                    continue
                b = ring_block(t, d)
                along(t, d, u, b).wait_recv()
                if goes(t + 1, d, u):
                    start(along(t + 1, d, u, b))
                start(across(c, t, d, u, b))
            if t == half - 1:
                projected = project(projected, c, u)
    for u in range(PIECES):
        own_across(other, u).wait_recv()
        for t in range(half):
            for d in range(2):
                if goes(t, d, u):
                    across(other, t, d, u, ring_block(t, d)).wait_recv()
        projected = project(projected, other, u)

    mixed[...] = projected.astype(BF16)
    stream = res[...].astype(F32) + projected
    y[...] = (stream * gain[...]).astype(BF16)
    shift = each * (col // each)

    def target_of(k, i):
        return each * lax.rem(col // each + chips + chips - k, chips) + i

    def slot_at(k):
        return k * each + lax.rem(col, each)

    def send_rows(k):
        for i in range(each):
            to = target_of(k, i)
            xs[to] = jnp.dot(pick[to], y[...], preferred_element_type=F32).astype(BF16)

            @pl.when(to != col)
            def _(k=k, to=to):
                remote(xs.at[to], xr.at[slot_at(k)], x_s.at[to], x_r.at[slot_at(k)], {"expert": to}).start()

            @pl.when(to == col)
            def _(k=k, to=to):
                xr[slot_at(k)] = xs[to]

    for t in range(half - 1):
        for d in range(2):
            send_rows(ring_block(t, d))
    send_rows(ring_block(half - 1, 0))
    send_rows(z)

    def wait_rows(k):
        for i in range(each):
            b = k * each + i
            src = lax.rem(b + shift, e)

            @pl.when(src != col)
            def _(b=b, src=src):
                remote(xs.at[0], xr.at[b], x_s.at[0], x_r.at[b], {"expert": src}).wait_recv()

    eye = lax.broadcasted_iota(jnp.int32, square, 0) == lax.broadcasted_iota(jnp.int32, square, 1)
    column = jnp.sum(stream * stream, axis=1, keepdims=True)
    flat = jnp.sum(jnp.where(eye, column, 0.0), axis=0, keepdims=True)
    sqs[...] = jnp.broadcast_to(flat, sqs.shape)
    for o in range(1, n):
        start(remote(sqs, sqr.at[o], sq_ss.at[o], sq_rs.at[o], {"sample": lax.rem(me + o, n)}))

    quarter = pown.shape[4]
    ff = 4 * quarter
    fetch_wg.wait()

    def chunk(d, t):
        return lax.rem(z + (chips + chips - 1 - t if d == 0 else 1 + t), chips)

    def partial(gq, dst, d, k):
        own = pl.ds(k * each, each)
        for side in range(2):
            lanes = pl.ds(pl.multiple_of(side * ff + gq * quarter, 128), quarter)
            tiles = {}
            for j, (low, high) in enumerate(spans()):
                lhs = xr[own, low:high, :].reshape(each * (high - low), features)
                got = jnp.dot(lhs, wg[j, :, lanes], preferred_element_type=F32)
                got = got.reshape(each, high - low, quarter)
                for tile in range(low // TILE, high // TILE):
                    piece = got[:, tile * TILE - low:(tile + 1) * TILE - low, :]
                    tiles.setdefault(tile, []).append((j, piece))
            for tile, parts in tiles.items():
                dst[d, own, side, tile * TILE:(tile + 1) * TILE, :] = merge_tile(tile, parts).astype(BF16)

    def pair(d, t):
        own = pl.ds(chunk(d, t) * each, each)
        return remote(psib.at[d, own], rsib.at[d, own], ps_s.at[d, t], ps_r.at[d, t], sibling)

    def hop(d, t, u, w):
        b = chunk(d, t) * each + u
        return remote(pown.at[d, b, w], rr.at[d, t, u, w], rs_s.at[d, t, u, w], rs_r.at[d, t, u, w], ways[d])

    def pair_sum(d, b, w):
        return pown[d, b, w].astype(F32) + rsib[d, b, w].astype(F32)

    def prepare(t):
        for d in range(2):
            partial(2 * other + d, psib, d, chunk(d, t))
            pair(d, t).start()
        for d in range(2):
            partial(2 * c + d, pown, d, chunk(d, t))

    def norm_factor():
        squares = sqs[...]
        for o in range(1, n):
            remote(
                sqs, sqr.at[o], sq_ss.at[o], sq_rs.at[o], {"sample": lax.rem(me + n - o, n)}
            ).wait_recv()
            squares = squares + sqr[o]
        factor = lax.rsqrt(squares / (features * n) + EPSILON)[0:1, :]
        for i in range(each):
            to = target_of(z, i)
            values = jnp.sum(pick[to].astype(F32) * factor, axis=1, keepdims=True)
            fsend[i] = jnp.broadcast_to(values, fsend.shape[1:])

            @pl.when(to != col)
            def _(i=i, to=to):
                place_at = lax.rem(col, each)
                remote(fsend.at[i], frecv.at[place_at], f_s.at[i], f_r.at[place_at], {"expert": to}).start()

            @pl.when(to == col)
            def _(i=i):
                frecv[lax.rem(col, each)] = fsend[i]

    def ring(t, carry):
        @pl.when(t < half)
        def _():
            wait_rows(chunk(0, t))

        @pl.when(t < half - 1)
        def _():
            wait_rows(chunk(1, t))

        prepare(t)
        for d in range(2):
            pair(d, t).wait_recv()
        for u in range(each):
            for w in range(2):
                for d in range(2):
                    b = chunk(d, t) * each + u

                    @pl.when(t == 0)
                    def _(d=d, b=b, w=w):
                        pown[d, b, w] = pair_sum(d, b, w).astype(BF16)

                    @pl.when(t > 0)
                    def _(d=d, b=b, u=u, w=w):
                        hop(d, t - 1, u, w).wait_recv()
                        value = pair_sum(d, b, w) + rr[d, t - 1, u, w].astype(F32)
                        pown[d, b, w] = value.astype(BF16)

                    hop(d, t, u, w).start()

        @pl.when(t == 1)
        def _():
            norm_factor()

        @pl.when(t == 2)
        def _():
            for copy in sent_before:
                copy.wait_send()

        return carry

    sent_before = list(sent)
    sent.clear()
    lax.fori_loop(0, chips - 1, ring, 0)
    wait_rows(z)
    prepare(chips - 1)
    for i in range(each):
        src = lax.rem(z * each + i + shift, e)

        @pl.when(src != col)
        def _(i=i, src=src):
            remote(fsend.at[0], frecv.at[i], f_s.at[0], f_r.at[i], {"expert": src}).wait_recv()

    for d in range(2):
        pair(d, chips - 1).wait_recv()

    def act_part(core, b, w):
        return act.at[core, b, w]

    def spread(d, t, u, w, b):
        ref = act_part(c, b, w)
        return remote(ref, ref, aa_s.at[d, t, u, w], aa_r.at[d, t, u, w], ways[d])

    def hand(core, d, t, u, w, b):
        ref = act_part(core, b, w)
        return remote(ref, ref, fw_s.at[d, t, u, w], fw_r.at[d, t, u, w], sibling)

    def own_hand(core, u, w):
        ref = act_part(core, z * each + u, w)
        return remote(ref, ref, me_sem.at[0, u, w], me_sem.at[1, u, w], sibling)

    for u in range(each):
        b = z * each + u
        factor = frecv[u][:, 0:1]
        for part_of in range(2):
            sums = []
            for w in range(2):
                hop(part_of, chips - 2, u, w).wait_recv()
                value = pair_sum(part_of, b, w) + rr[part_of, chips - 2, u, w].astype(F32)
                sums.append(value * factor)
            gate, up = sums
            act[c, b, part_of] = (gate / (1.0 + jnp.exp(-gate)) * up).astype(BF16)
            for d in range(2):
                if goes(0, d, u):
                    start(spread(d, 0, u, part_of, b))
            start(own_hand(c, u, part_of))
    fetch_wd.wait()

    def finish(slots):
        tiles = {}
        count = len(slots)
        for j, (low, high) in enumerate(spans()):
            got = None
            for core in range(2):
                halves = [
                    jnp.concatenate([act[core, b, w, low:high, :] for b in slots], axis=0) for w in range(2)
                ]
                lhs = jnp.concatenate(halves, axis=1)
                depth = slice(core * 2 * quarter, (core + 1) * 2 * quarter)
                term = jnp.dot(lhs, wd[j, depth, :], preferred_element_type=F32)
                got = term if got is None else got + term
            got = got.reshape(count, high - low, got.shape[1])
            for tile in range(low // TILE, high // TILE):
                piece = got[:, tile * TILE - low:(tile + 1) * TILE - low, :]
                tiles.setdefault(tile, []).append((j, piece))
        done = {tile: merge_tile(tile, parts).astype(BF16) for tile, parts in tiles.items()}
        for i, b in enumerate(slots):
            for tile, value in done.items():
                osend[b, tile * TILE:(tile + 1) * TILE, :] = value[i]
            target = lax.rem(b + shift, e)

            @pl.when(target != col)
            def _(b=b, target=target):
                remote(osend.at[b], oret.at[col], o_s.at[b], o_r.at[col], {"expert": target}).start()

            @pl.when(target == col)
            def _(b=b):
                oret[col] = osend[b]

    def complete(pending):
        for b, copies in pending:
            for copy in copies:
                copy.wait_recv()
        finish([b for b, copies in pending])

    def drain(t, carry):
        for d in range(2):
            pair(d, t).wait_send()

            @pl.when(t < chips - 1)
            def _(d=d):
                for u in range(each):
                    for w in range(2):
                        hop(d, t, u, w).wait_send()

        return carry

    def drain_rows(b, carry):
        @pl.when(b != col)
        def _():
            remote(xs.at[b], xr.at[0], x_s.at[b], x_r.at[0], {"expert": b}).wait_send()

        return carry

    def drain_factor():
        for i in range(each):
            to = target_of(z, i)

            @pl.when(to != col)
            def _(i=i, to=to):
                remote(fsend.at[i], frecv.at[0], f_s.at[i], f_r.at[0], {"expert": to}).wait_send()

    def step_chunks(t):
        return [ring_block(t, 0), ring_block(t, 1)] if t < half - 1 else [ring_block(t, 0)]

    def combine(total, ks):
        for k in ks:
            for i in range(each):
                src = target_of(k, i)

                @pl.when(src != col)
                def _(src=src):
                    remote(osend.at[0], oret.at[src], o_s.at[0], o_r.at[src], {"expert": src}).wait_recv()

            p = lax.rem(col // each + chips + chips - k, chips)
            back = oret[pl.ds(p * each, each)].reshape(each * unit, out.shape[1])
            total = total + jnp.dot(chi[p], back, preferred_element_type=F32)
            total = total + jnp.dot(clo[p], back, preferred_element_type=F32)
        return total

    total = jnp.zeros(out.shape, F32)
    pending = [(z * each + u, [own_hand(other, u, w) for w in range(2)]) for u in range(each)]
    for t in range(half):
        if t == half - 1:
            complete(pending)
            pending = []
            total = combine(total, [z])
            for early_step in range(half - 3):
                total = combine(total, step_chunks(early_step))
        fresh = []
        for u in range(each):
            for d in range(2):
                if not goes(t, d, u):
                    continue
                fresh.append(
                    (ring_block(t, d) * each + u, [hand(other, d, t, u, w, ring_block(t, d) * each + u) for w in range(2)])
                )
            for w in range(2):
                for d in range(2):
                    if not goes(t, d, u):
                        continue
                    b = ring_block(t, d) * each + u
                    spread(d, t, u, w, b).wait_recv()
                    if goes(t + 1, d, u):
                        start(spread(d, t + 1, u, w, b))
                    start(hand(c, d, t, u, w, b))
        if pending:
            complete(pending)
        if t == 0:
            lax.fori_loop(0, chips, drain, 0)
            lax.fori_loop(0, e, drain_rows, 0)
            drain_factor()
        if t == half - 1 and half > 2:
            total = combine(total, step_chunks(half - 3))
        pending = fresh
    complete(pending)

    for t in range(max(half - 2, 0), half):
        total = combine(total, step_chunks(t))
    out[...] = total.astype(BF16)

    for copy in sent:
        copy.wait_send()

    def drain_out(b, carry):
        target = lax.rem(b + shift, e)

        @pl.when(target != col)
        def _():
            remote(osend.at[b], oret.at[col], o_s.at[b], o_r.at[col], {"expert": target}).wait_send()

        return carry

    lax.fori_loop(0, e, drain_out, 0)


def on_device(
    n, e, queries, prompt_kv, gen_kv, gen_lengths, out_proj, residual, norm_gain,
    w_gate_up, w_down, routes, route_probs,
):
    prompts = queries.shape[0]
    rows = prompts * n
    features = residual.shape[2]
    out_features = w_down.shape[2]
    chips = n // 2
    half = chips // 2
    each = e // chips
    unit = -(-EXP_COL * CAP // TILE) * TILE
    heads = queries.shape[2] // HDIM
    topk = routes.shape[2]
    width = HERE * GROUPS * HDIM
    wide = HERE * HDIM
    tokens, gen = prompt_kv.shape[1], gen_kv.shape[2]
    quarter = w_gate_up.shape[2] // 8
    table = 128
    hbm = pl.BlockSpec(memory_space=pltpu.HBM)
    vmem = pl.BlockSpec(memory_space=pltpu.VMEM)
    dma = pltpu.SemaphoreType.DMA
    buf = pltpu.VMEM
    mixed, expert_out = pl.pallas_call(
        functools.partial(kernel, n, e),
        out_shape=(
            pltpu.VMEM((rows, features), BF16),
            pltpu.VMEM((rows, out_features), BF16),
        ),
        in_specs=[hbm] * 11,
        out_specs=(vmem, vmem),
        scratch_shapes=[
            buf((prompts, heads * HDIM), BF16),
            buf((prompts, heads, HDIM), F32),
            buf((prompts, heads, HDIM), BF16),
            buf((1, prompts), jnp.int32),
            buf((rows, features), BF16),
            buf((1, features), F32),
            buf((prompts, topk, n), jnp.int32),
            buf((prompts, topk, n), F32),
            buf((prompts, 2, tokens, 2 * wide), BF16),
            buf((prompts, gen, gen_kv.shape[3]), BF16),
            buf((prompts, 2, (HERE + 1) * GROUPS, HDIM), BF16),
            buf((n, HERE * GROUPS, HDIM), BF16),
            buf((n, (HERE + 1) * GROUPS, HDIM), BF16),
            buf((n, tokens, 2 * wide), BF16),
            buf((2, width, features), BF16),
            buf(w_gate_up.shape, BF16),
            buf(w_down.shape, BF16),
            buf((HERE, n * GROUPS, HDIM), F32),
            buf((HERE, n * GROUPS, HDIM), F32),
            buf((HERE, n * GROUPS, HDIM), F32),
            buf((HERE, n * GROUPS, HDIM), BF16),
            buf((2, rows, width), BF16),
            buf((8, rows), F32),
            buf((n, 8, rows), F32),
            buf((rows, table), BF16),
            buf((e, unit, rows), BF16),
            buf((chips, rows, each * unit), BF16),
            buf((chips, rows, each * unit), BF16),
            buf((rows, features), BF16),
            buf((e, unit, features), BF16),
            buf((e, unit, features), BF16),
            buf((2, e, 2, unit, quarter), BF16),
            buf((2, e, 2, unit, quarter), BF16),
            buf((2, e, 2, unit, quarter), BF16),
            buf((2, chips - 1, each, 2, unit, quarter), BF16),
            buf((2, e, 2, unit, quarter), BF16),
            buf((e, unit, out_features), BF16),
            buf((e, unit, out_features), BF16),
            buf((each, unit, HDIM), F32),
            buf((each, unit, HDIM), F32),
            dma((17,)),
            dma((3, n)),
            dma((3, n)),
            dma((2, half, PIECES)),
            dma((2, half, PIECES)),
            dma((2, half, PIECES)),
            dma((2, half, PIECES)),
            dma((2, PIECES)),
            dma((n,)),
            dma((n,)),
            dma((e,)),
            dma((e,)),
            dma((2, chips)),
            dma((2, chips)),
            dma((2, chips - 1, each, 2)),
            dma((2, chips - 1, each, 2)),
            dma((2, half, each, 2)),
            dma((2, half, each, 2)),
            dma((2, half, each, 2)),
            dma((2, half, each, 2)),
            dma((2, each, 2)),
            dma((e,)),
            dma((e,)),
            dma((each,)),
            dma((each,)),
        ],
        compiler_params=pltpu.CompilerParams(
            collective_id=0, has_side_effects=True, vmem_limit_bytes=56 << 20
        ),
        name="decode_step",
    )(
        queries.reshape(prompts, heads * HDIM),
        gen_lengths.T,
        prompt_kv,
        gen_kv.reshape(prompts, gen, gen_kv.shape[3]),
        out_proj.reshape(2, width, features),
        residual.reshape(rows, features),
        norm_gain.reshape(1, features),
        jnp.swapaxes(routes, 1, 2),
        jnp.swapaxes(route_probs, 1, 2),
        w_gate_up,
        w_down,
    )
    shape = (prompts, n, features)
    return (mixed.reshape(shape), expert_out.reshape(shape))


def solution(mesh):
    placed = (
        P("expert", "sample", None),
        P("expert", "sample", None),
        P("expert", "sample", None, None),
        P("expert", "sample"),
        P(None, "sample"),
        P("expert", None, "sample"),
        P("sample"),
        P("expert", "sample", None),
        P("expert", None, "sample"),
        P("expert", None, None),
        P("expert", None, None),
    )
    return jax.shard_map(
        functools.partial(on_device, mesh.shape["sample"], mesh.shape["expert"]),
        mesh=mesh,
        in_specs=placed,
        out_specs=(P("expert", None, "sample"), P("expert", None, "sample")),
        check_vma=False,
    )
```

```python
import functools

import jax
import jax.numpy as jnp
from jax import lax
from jax.experimental import pallas as pl
from jax.experimental.pallas import tpu as pltpu
from jax.sharding import PartitionSpec as P

MESH = pl.DeviceIdType.MESH
HDIM = 128
GROUPS = 16
KVHEADS = 4
HERE = 2
EXP_COL = 3
CAP = 26
TILE = 16
PIECES = 4
NEGATIVE = -1e30
EPSILON = 1e-06
F32 = jnp.float32
BF16 = jnp.bfloat16
NT = (((1,), (1,)), ((), ()))


def remote(src, dst, send, recv, device):
    return pltpu.make_async_remote_copy(
        src_ref=src, dst_ref=dst, send_sem=send, recv_sem=recv, device_id=device, device_id_type=MESH
    )


def spans():
    out = []
    for j in range(EXP_COL):
        low = CAP * j // TILE * TILE
        high = -(-CAP * (j + 1) // TILE) * TILE
        out.append((low, high))
    return out


def merge_tile(tile, parts):
    if len(parts) == 1:
        return parts[0][1]
    (first, a), (second, b) = parts
    shape = (1,) * (a.ndim - 2) + (TILE, 1)
    rows = lax.broadcasted_iota(jnp.int32, shape, a.ndim - 2) + tile * TILE
    return jnp.where(rows < CAP * (first + 1), a, b)


def token_order(chips):
    return [0] + sorted(range(1, chips), key=lambda d: -min(d, chips - d))


def kernel(
    n, e,
    q_in, lens_in, kv, gkv, wo, res_in, gain_in, ids_in, probs_in, wgu, wdn,
    mixed, out,
    qraw, qwide, q, lens, res, gain, ids, probs, kvv, gv, gmsg, rq, rm, rkv, wov, wg, wd, ost, mst, lst, obuf, att, sqs, sqr,
    place, pick, chi, clo, y, xs, xr, pown, psib, rsib, rr, act, osend, oret, fsend, frecv,
    lsem, ex_s, ex_r, ag_s, ag_r, sib_s, sib_r, own_sem, sq_ss, sq_rs,
    x_s, x_r, ps_s, ps_r, rs_s, rs_r, aa_s, aa_r, fw_s, fw_r, me_sem, o_s, o_r, f_s, f_r,
):
    chips = n // 2
    half = chips // 2
    each = e // chips
    me = lax.axis_index("sample")
    col = lax.axis_index("expert")
    z, c = me // 2, lax.rem(me, 2)
    other = 1 - c
    wide = HERE * HDIM
    right = {"sample": 2 * lax.rem(z + 1, chips) + c}
    left = {"sample": 2 * lax.rem(z + chips - 1, chips) + c}
    ways = (right, left)
    sibling = {"sample": 2 * z + other}
    unit = xs.shape[1]
    rows_all, features = res.shape
    sent = []

    def start(copy):
        copy.start()
        sent.append(copy)

    def fetch(src, dst, k):
        copy = pltpu.make_async_copy(src, dst, lsem.at[k])
        copy.start()
        return copy

    small = [
        fetch(a, b, 7 + i)
        for i, (a, b) in enumerate(
            ((q_in, qraw), (lens_in, lens), (res_in, res), (gain_in, gain), (ids_in, ids), (probs_in, probs))
        )
    ]
    fetch_g = fetch(gkv, gv, 1)
    fetch_kv = []
    for hp in range(2):
        for side in range(2):
            begin = (2 * side + hp) * HERE * HDIM
            fetch_kv.append(
                fetch(
                    kv.at[:, :, begin:begin + HERE * HDIM],
                    kvv.at[:, hp, :, side * HERE * HDIM:(side + 1) * HERE * HDIM],
                    13 + 2 * hp + side,
                )
            )

    barrier = pltpu.get_barrier_semaphore()

    def greet_sample(o, carry):
        pl.semaphore_signal(barrier, inc=1, device_id={"sample": lax.rem(me + o, n)}, device_id_type=MESH)
        return carry

    def greet_expert(o, carry):
        pl.semaphore_signal(barrier, inc=1, device_id={"expert": lax.rem(col + o, e)}, device_id_type=MESH)
        return carry

    lax.fori_loop(1, n, greet_sample, 0)
    lax.fori_loop(1, e, greet_expert, 0)

    for copy in small:
        copy.wait()
    for h in range(q.shape[1]):
        qwide[:, h, :] = qraw[:, h * HDIM:(h + 1) * HDIM].astype(F32)
    q[...] = qwide[...].astype(BF16)
    prompts = q.shape[0]
    gen = gv.shape[1]
    scale = HDIM ** (-0.5)
    for copy in fetch_kv:
        copy.wait()
    pl.semaphore_wait(barrier, n - 1 + e - 1)

    order = token_order(chips)
    where_of = {d: i for i, d in enumerate(order)}

    def q_pair(p, hp):
        return q.at[p, pl.ds(pl.multiple_of(hp * HERE * GROUPS, HERE * GROUPS), HERE * GROUPS)], rq.at[me]

    def m_pair(p, hp):
        return gmsg.at[p, hp], rm.at[me]

    def kv_pair(p, hp, slot):
        return kvv.at[p, hp], rkv.at[slot]

    def exchange(kind, dz, hp):
        p = lax.rem(z + dz, chips)
        slot = 2 * where_of[(chips - dz) % chips] + c
        src, dst = (q_pair(p, hp), m_pair(p, hp), kv_pair(p, hp, slot))[kind]
        target = {"sample": 2 * p + hp}
        start(remote(src, dst, ex_s.at[kind, 2 * dz + (hp if dz else 0)], ex_r.at[kind, slot], target))

    early = order[1:half]

    def send_all(kinds, distances):
        for dz in distances:
            for hp in range(2):
                for kind in kinds:
                    exchange(kind, dz, hp)

    send_all((2,), early)
    send_all((0,), order[1:])
    for kind in (0, 2):
        exchange(kind, 0, other)
    fetch_g.wait()
    tall = prompts * GROUPS
    of_row = lax.broadcasted_iota(jnp.int32, (tall, prompts), 0) // GROUPS
    is_row = of_row == lax.broadcasted_iota(jnp.int32, (tall, prompts), 1)
    length = jnp.sum(jnp.where(is_row, lens[...].astype(F32), 0.0), axis=1, keepdims=True)
    lane = lax.broadcasted_iota(jnp.int32, (tall, HDIM), 1)
    for hp in range(2):
        stats = jnp.zeros((tall, HDIM), F32)
        for hl in range(HERE):
            h = hp * HERE + hl
            query = q[:, h * GROUPS:(h + 1) * GROUPS, :].reshape(tall, HDIM)
            keys = gv[:, :, h * HDIM:(h + 1) * HDIM].reshape(prompts * gen, HDIM)
            vals = gv[:, :, (KVHEADS + h) * HDIM:(KVHEADS + h + 1) * HDIM].reshape(prompts * gen, HDIM)
            scores = lax.dot_general(query, keys, NT, preferred_element_type=F32) * scale
            row = lax.broadcasted_iota(jnp.int32, scores.shape, 0) // GROUPS
            at_key = (lax.broadcasted_iota(jnp.int32, scores.shape, 1) - row * gen).astype(F32)
            scores = jnp.where(jnp.logical_and(at_key >= 0.0, at_key < length), scores, NEGATIVE)
            highest = jnp.max(scores, axis=1, keepdims=True)
            weight = jnp.exp(scores - highest)
            total = jnp.sum(weight, axis=1, keepdims=True)
            got = jnp.dot(weight.astype(BF16), vals, preferred_element_type=F32) / total
            gmsg[:, hp, hl * GROUPS:(hl + 1) * GROUPS, :] = got.astype(BF16).reshape(prompts, GROUPS, HDIM)
            level = highest + jnp.log(total)
            for k in range(3):
                part = level.astype(BF16).astype(F32)
                level = level - part
                stats = jnp.where(lane == 3 * hl + k, part, stats)
        gmsg[:, hp, HERE * GROUPS:, :] = stats.astype(BF16).reshape(prompts, GROUPS, HDIM)
    exchange(1, 0, other)
    send_all((1,), order[1:])
    send_all((2,), order[half:])
    local = []
    for kind, (src, dst) in enumerate((q_pair(z, c), m_pair(z, c), kv_pair(z, c, c))):
        local.append(fetch(src, dst, kind))
    fetch_wo = fetch(wo, wov, 4)
    fetch_wg = fetch(wgu, wg, 5)
    fetch_wd = fetch(wdn, wd, 6)

    experts = place.shape[1]
    topk = ids.shape[1]
    named = jnp.zeros((topk, rows_all), F32)
    given = jnp.zeros((topk, rows_all), F32)
    for p in range(prompts):
        sample = lax.broadcasted_iota(jnp.int32, (n, rows_all), 0)
        there = lax.broadcasted_iota(jnp.int32, (n, rows_all), 1) == sample + p * n
        there = jnp.where(there, 1.0, 0.0).astype(BF16)
        named = named + jnp.dot(ids[p].astype(F32).astype(BF16), there, preferred_element_type=F32)
        rest = probs[p]
        for k in range(3):
            part = rest.astype(BF16)
            rest = rest - part.astype(F32)
            given = given + jnp.dot(part, there, preferred_element_type=F32)
    lane = lax.broadcasted_iota(jnp.int32, (rows_all, experts), 1)
    expert_row = lax.broadcasted_iota(jnp.int32, (experts, rows_all), 0).astype(F32)
    hits = jnp.zeros((experts, rows_all), F32)
    share_t = jnp.zeros((experts, rows_all), F32)
    for k in range(topk):
        same = expert_row == named[k:k + 1, :]
        hits = hits + jnp.where(same, 1.0, 0.0)
        share_t = share_t + jnp.where(same, given[k:k + 1, :], 0.0)
    square = (rows_all, rows_all)
    row_index = lax.broadcasted_iota(jnp.int32, square, 0)
    lane_index = lax.broadcasted_iota(jnp.int32, square, 1)
    above = jnp.where(row_index < lane_index, 1.0, 0.0).astype(BF16)
    eye_bf = jnp.where(row_index == lane_index, 1.0, 0.0).astype(BF16)
    before = jnp.dot(hits.astype(BF16), above, preferred_element_type=F32)
    place_t = jnp.where(hits > 0.5, before, -1.0).astype(BF16)
    place[...] = lax.dot_general(eye_bf, place_t, NT, preferred_element_type=F32).astype(BF16)
    at = lax.broadcasted_iota(jnp.int32, (e, unit, experts), 1)
    local_expert = jnp.zeros((e, unit, experts), jnp.int32)
    for j in range(1, EXP_COL):
        local_expert = local_expert + jnp.where(at >= CAP * j, 1, 0)
    slot_of = (at - CAP * local_expert).astype(F32)
    owner = lax.broadcasted_iota(jnp.int32, (e, unit, experts), 0) * EXP_COL + local_expert
    on_lane = lax.broadcasted_iota(jnp.int32, (e, unit, experts), 2)
    table = jnp.where(owner == on_lane, 1.0, 0.0).astype(BF16).reshape(e * unit, experts)
    seen = jnp.dot(table, place_t, preferred_element_type=F32)
    pick[...] = jnp.where(seen.reshape(e, unit, rows_all) == slot_of[:, :, :rows_all], 1.0, 0.0).astype(BF16)
    slot_table = jnp.where(on_lane == 0, slot_of, 0.0).astype(BF16).reshape(e * unit, experts)
    first_lane = jnp.where(lane == 0, 1.0, 0.0).astype(BF16)
    share_parts = []
    for k in range(2):
        part_t = share_t.astype(BF16)
        share_t = share_t - part_t.astype(F32)
        share_parts.append(lax.dot_general(eye_bf, part_t, NT, preferred_element_type=F32).astype(BF16))
    for p in range(chips):
        band = slice(p * each * unit, (p + 1) * each * unit)
        slot_row = lax.dot_general(first_lane, slot_table[band], NT, preferred_element_type=F32)
        placed = lax.dot_general(place[...], table[band], NT, preferred_element_type=F32)
        chosen = placed == slot_row
        for ref, part in zip((chi, clo), share_parts):
            spread_part = lax.dot_general(part, table[band], NT, preferred_element_type=F32)
            ref[p] = jnp.where(chosen, spread_part, 0.0).astype(BF16)

    for copy in local:
        copy.wait()

    def arrived(kind, slot):
        if kind == 0:
            src, dst = q_pair(0, 0)
        elif kind == 1:
            src, dst = m_pair(0, 0)
        else:
            src, dst = kv_pair(0, 0, slot)
        remote(src, dst, ex_s.at[kind, 1], ex_r.at[kind, slot], sibling).wait_recv()

    def arrive_all(kinds, low, high):
        def body(i, carry):
            for kind in kinds:
                arrived(kind, i)
            return carry

        lax.fori_loop(low, high, body, 0)

    for kind in range(3):
        arrived(kind, other)
    arrive_all((0, 1), 2, n)
    first = n // 2
    arrive_all((2,), 2, first)
    block = min(8, n)
    slab = block * GROUPS

    def absorb(h, i, low, high, highest, total, acc):
        own = pl.ds(i * block, block)
        query = rq[own, h * GROUPS:(h + 1) * GROUPS, :].reshape(slab, HDIM)
        lanes = slice(h * HDIM, (h + 1) * HDIM)
        count = (high - low) * rkv.shape[1]
        keys = rkv[low:high, :, lanes].reshape(count, HDIM)
        vals = rkv[low:high, :, wide + h * HDIM:wide + (h + 1) * HDIM].reshape(count, HDIM)
        scores = lax.dot_general(query, keys, NT, preferred_element_type=F32) * scale
        peak = jnp.maximum(highest, jnp.max(scores, axis=1, keepdims=True))
        kept = jnp.exp(highest - peak)
        weight = jnp.exp(scores - peak)
        total = total * kept + jnp.sum(weight, axis=1, keepdims=True)
        acc = acc * kept + jnp.dot(weight.astype(BF16), vals, preferred_element_type=F32)
        return peak, total, acc

    def slab_rows(i):
        return pl.ds(pl.multiple_of(i * slab, slab), slab)

    for h in range(HERE):

        def stage_one(i, carry, h=h):
            own = pl.ds(i * block, block)
            stats = rm[own, HERE * GROUPS:, :].reshape(slab, HDIM).astype(F32)
            level = stats[:, 3 * h:3 * h + 1] + stats[:, 3 * h + 1:3 * h + 2] + stats[:, 3 * h + 2:3 * h + 3]
            acc = rm[own, h * GROUPS:(h + 1) * GROUPS, :].reshape(slab, HDIM).astype(F32)
            peak, total, acc = absorb(h, i, 0, first, level, jnp.ones((slab, 1), F32), acc)
            mst[h, slab_rows(i), :] = jnp.broadcast_to(peak, (slab, HDIM))
            lst[h, slab_rows(i), :] = jnp.broadcast_to(total, (slab, HDIM))
            ost[h, slab_rows(i), :] = acc
            return carry

        lax.fori_loop(0, n // block, stage_one, 0)

    count = n * GROUPS
    r = lax.broadcasted_iota(jnp.int32, (count, count), 0)
    k = lax.broadcasted_iota(jnp.int32, (count, count), 1)
    swap = jnp.where(k == (lax.rem(r, n) * GROUPS + r // n), 1.0, 0.0).astype(BF16)
    at_rows = pl.ds(pl.multiple_of(z * n, n), n)
    width = HERE * GROUPS * HDIM
    cut = width // PIECES
    per_head = PIECES // HERE

    def part(core, b, u):
        return att.at[core, pl.ds(pl.multiple_of(b * n, n), n), u * cut:(u + 1) * cut]

    def goes(t, d, u):
        return t < half - 1 or (t == half - 1 and u % 2 == d)

    def ring_block(t, d):
        return lax.rem(z + (chips - 1 - t if d == 0 else 1 + t), chips)

    def along(t, d, u, b):
        ref = part(c, b, u)
        return remote(ref, ref, ag_s.at[d, t, u], ag_r.at[d, t, u], ways[d])

    def across(core, t, d, u, b):
        ref = part(core, b, u)
        return remote(ref, ref, sib_s.at[d, t, u], sib_r.at[d, t, u], sibling)

    def own_across(core, u):
        ref = part(core, z, u)
        return remote(ref, ref, own_sem.at[0, u], own_sem.at[1, u], sibling)

    arrive_all((2,), first, n)
    for h in range(HERE):

        def stage_two(i, carry, h=h):
            peak = mst[h, slab_rows(i), 0:1]
            total = lst[h, slab_rows(i), 0:1]
            peak, total, acc = absorb(h, i, first, n, peak, total, ost[h, slab_rows(i), :])
            obuf[h, slab_rows(i), :] = (acc / total).astype(BF16)
            return carry

        lax.fori_loop(0, n // block, stage_two, 0)
        swapped = jnp.dot(swap, obuf[h], preferred_element_type=F32).astype(BF16)
        for g in range(GROUPS):
            begin = (h * GROUPS + g) * HDIM
            att[c, at_rows, begin:begin + HDIM] = swapped[g * n:(g + 1) * n, :]
        for u in range(h * per_head, (h + 1) * per_head):
            for d in range(2):
                if goes(0, d, u):
                    start(along(0, d, u, z))
        for u in range(h * per_head, (h + 1) * per_head):
            start(own_across(c, u))

    fetch_wo.wait()
    projected = jnp.zeros((rows_all, features), F32)

    def project(acc, core, u):
        lanes = slice(u * cut, (u + 1) * cut)
        return acc + jnp.dot(att[core, :, lanes], wov[core, lanes, :], preferred_element_type=F32)

    for t in range(half):
        for u in range(PIECES):
            for d in range(2):
                if not goes(t, d, u):
                    continue
                b = ring_block(t, d)
                along(t, d, u, b).wait_recv()
                if goes(t + 1, d, u):
                    start(along(t + 1, d, u, b))
                start(across(c, t, d, u, b))
            if t == half - 1:
                projected = project(projected, c, u)
    for u in range(PIECES):
        own_across(other, u).wait_recv()
        for t in range(half):
            for d in range(2):
                if goes(t, d, u):
                    across(other, t, d, u, ring_block(t, d)).wait_recv()
        projected = project(projected, other, u)

    mixed[...] = projected.astype(BF16)
    stream = res[...].astype(F32) + projected
    y[...] = (stream * gain[...]).astype(BF16)
    shift = each * (col // each)

    def target_of(k, i):
        return each * lax.rem(col // each + chips + chips - k, chips) + i

    def slot_at(k):
        return k * each + lax.rem(col, each)

    def send_rows(k):
        for i in range(each):
            to = target_of(k, i)
            xs[to] = jnp.dot(pick[to], y[...], preferred_element_type=F32).astype(BF16)

            @pl.when(to != col)
            def _(k=k, to=to):
                remote(xs.at[to], xr.at[slot_at(k)], x_s.at[to], x_r.at[slot_at(k)], {"expert": to}).start()

            @pl.when(to == col)
            def _(k=k, to=to):
                xr[slot_at(k)] = xs[to]

    for t in range(half - 1):
        for d in range(2):
            send_rows(ring_block(t, d))
    send_rows(ring_block(half - 1, 0))
    send_rows(z)

    def wait_rows(k):
        for i in range(each):
            b = k * each + i
            src = lax.rem(b + shift, e)

            @pl.when(src != col)
            def _(b=b, src=src):
                remote(xs.at[0], xr.at[b], x_s.at[0], x_r.at[b], {"expert": src}).wait_recv()

    eye = lax.broadcasted_iota(jnp.int32, square, 0) == lax.broadcasted_iota(jnp.int32, square, 1)
    column = jnp.sum(stream * stream, axis=1, keepdims=True)
    flat = jnp.sum(jnp.where(eye, column, 0.0), axis=0, keepdims=True)
    sqs[...] = jnp.broadcast_to(flat, sqs.shape)
    for o in range(1, n):
        start(remote(sqs, sqr.at[o], sq_ss.at[o], sq_rs.at[o], {"sample": lax.rem(me + o, n)}))

    quarter = pown.shape[4]
    ff = 4 * quarter
    fetch_wg.wait()

    def chunk(d, t):
        return lax.rem(z + (chips + chips - 1 - t if d == 0 else 1 + t), chips)

    def partial(gq, dst, d, k):
        own = pl.ds(k * each, each)
        for side in range(2):
            lanes = pl.ds(pl.multiple_of(side * ff + gq * quarter, 128), quarter)
            tiles = {}
            for j, (low, high) in enumerate(spans()):
                lhs = xr[own, low:high, :].reshape(each * (high - low), features)
                got = jnp.dot(lhs, wg[j, :, lanes], preferred_element_type=F32)
                got = got.reshape(each, high - low, quarter)
                for tile in range(low // TILE, high // TILE):
                    piece = got[:, tile * TILE - low:(tile + 1) * TILE - low, :]
                    tiles.setdefault(tile, []).append((j, piece))
            for tile, parts in tiles.items():
                dst[d, own, side, tile * TILE:(tile + 1) * TILE, :] = merge_tile(tile, parts).astype(BF16)

    def pair(d, t):
        own = pl.ds(chunk(d, t) * each, each)
        return remote(psib.at[d, own], rsib.at[d, own], ps_s.at[d, t], ps_r.at[d, t], sibling)

    def hop(d, t, u, w):
        b = chunk(d, t) * each + u
        return remote(pown.at[d, b, w], rr.at[d, t, u, w], rs_s.at[d, t, u, w], rs_r.at[d, t, u, w], ways[d])

    def pair_sum(d, b, w):
        return pown[d, b, w].astype(F32) + rsib[d, b, w].astype(F32)

    def job(i, t):
        d = i % 2
        if i < 2:
            partial(2 * other + d, psib, d, chunk(d, t))
            pair(d, t).start()
        else:
            partial(2 * c + d, pown, d, chunk(d, t))

    def norm_factor():
        squares = sqs[...]
        for o in range(1, n):
            remote(
                sqs, sqr.at[o], sq_ss.at[o], sq_rs.at[o], {"sample": lax.rem(me + n - o, n)}
            ).wait_recv()
            squares = squares + sqr[o]
        factor = lax.rsqrt(squares / (features * n) + EPSILON)[0:1, :]
        for i in range(each):
            to = target_of(z, i)
            values = jnp.sum(pick[to].astype(F32) * factor, axis=1, keepdims=True)
            fsend[i] = jnp.broadcast_to(values, fsend.shape[1:])

            @pl.when(to != col)
            def _(i=i, to=to):
                place_at = lax.rem(col, each)
                remote(fsend.at[i], frecv.at[place_at], f_s.at[i], f_r.at[place_at], {"expert": to}).start()

            @pl.when(to == col)
            def _(i=i):
                frecv[lax.rem(col, each)] = fsend[i]

    def ring(t, carry):
        for d in range(2):
            pair(d, t).wait_recv()
        for u, w in [(u, w) for u in range(each) for w in range(2)]:
            for d in range(2):
                b = chunk(d, t) * each + u

                @pl.when(t == 0)
                def _(d=d, b=b, w=w):
                    pown[d, b, w] = pair_sum(d, b, w).astype(BF16)

                @pl.when(t > 0)
                def _(d=d, b=b, u=u, w=w):
                    hop(d, t - 1, u, w).wait_recv()
                    value = pair_sum(d, b, w) + rr[d, t - 1, u, w].astype(F32)
                    pown[d, b, w] = value.astype(BF16)

                hop(d, t, u, w).start()

        @pl.when(t + 1 < half)
        def _():
            wait_rows(chunk(0, t + 1))

        @pl.when(t + 1 < half - 1)
        def _():
            wait_rows(chunk(1, t + 1))

        @pl.when(t + 1 == chips - 1)
        def _():
            wait_rows(z)

        for i in range(4):
            job(i, t + 1)

        @pl.when(t == 1)
        def _():
            norm_factor()

        @pl.when(t == 2)
        def _():
            for copy in sent_before:
                copy.wait_send()

        return carry

    sent_before = list(sent)
    sent.clear()
    wait_rows(chunk(0, 0))
    wait_rows(chunk(1, 0))
    for i in range(4):
        job(i, 0)
    lax.fori_loop(0, chips - 1, ring, 0)
    for i in range(each):
        src = lax.rem(z * each + i + shift, e)

        @pl.when(src != col)
        def _(i=i, src=src):
            remote(fsend.at[0], frecv.at[i], f_s.at[0], f_r.at[i], {"expert": src}).wait_recv()

    for d in range(2):
        pair(d, chips - 1).wait_recv()

    def act_part(core, b, w):
        return act.at[core, b, w]

    def spread(d, t, u, w, b):
        ref = act_part(c, b, w)
        return remote(ref, ref, aa_s.at[d, t, u, w], aa_r.at[d, t, u, w], ways[d])

    def hand(core, d, t, u, w, b):
        ref = act_part(core, b, w)
        return remote(ref, ref, fw_s.at[d, t, u, w], fw_r.at[d, t, u, w], sibling)

    def own_hand(core, u, w):
        ref = act_part(core, z * each + u, w)
        return remote(ref, ref, me_sem.at[0, u, w], me_sem.at[1, u, w], sibling)

    for u in range(each):
        b = z * each + u
        factor = frecv[u][:, 0:1]
        for part_of in range(2):
            sums = []
            for w in range(2):
                hop(part_of, chips - 2, u, w).wait_recv()
                value = pair_sum(part_of, b, w) + rr[part_of, chips - 2, u, w].astype(F32)
                sums.append(value * factor)
            gate, up = sums
            act[c, b, part_of] = (gate / (1.0 + jnp.exp(-gate)) * up).astype(BF16)
            for d in range(2):
                if goes(0, d, u):
                    start(spread(d, 0, u, part_of, b))
            start(own_hand(c, u, part_of))
    fetch_wd.wait()

    def finish(slots):
        tiles = {}
        count = len(slots)
        for j, (low, high) in enumerate(spans()):
            got = None
            for core in range(2):
                halves = [
                    jnp.concatenate([act[core, b, w, low:high, :] for b in slots], axis=0) for w in range(2)
                ]
                lhs = jnp.concatenate(halves, axis=1)
                depth = slice(core * 2 * quarter, (core + 1) * 2 * quarter)
                term = jnp.dot(lhs, wd[j, depth, :], preferred_element_type=F32)
                got = term if got is None else got + term
            got = got.reshape(count, high - low, got.shape[1])
            for tile in range(low // TILE, high // TILE):
                piece = got[:, tile * TILE - low:(tile + 1) * TILE - low, :]
                tiles.setdefault(tile, []).append((j, piece))
        done = {tile: merge_tile(tile, parts).astype(BF16) for tile, parts in tiles.items()}
        for i, b in enumerate(slots):
            for tile, value in done.items():
                osend[b, tile * TILE:(tile + 1) * TILE, :] = value[i]
            target = lax.rem(b + shift, e)

            @pl.when(target != col)
            def _(b=b, target=target):
                remote(osend.at[b], oret.at[col], o_s.at[b], o_r.at[col], {"expert": target}).start()

            @pl.when(target == col)
            def _(b=b):
                oret[col] = osend[b]

    def complete(pending):
        for b, copies in pending:
            for copy in copies:
                copy.wait_recv()
        finish([b for b, copies in pending])

    def drain(t, carry):
        for d in range(2):
            pair(d, t).wait_send()

            @pl.when(t < chips - 1)
            def _(d=d):
                for u in range(each):
                    for w in range(2):
                        hop(d, t, u, w).wait_send()

        return carry

    def drain_rows(b, carry):
        @pl.when(b != col)
        def _():
            remote(xs.at[b], xr.at[0], x_s.at[b], x_r.at[0], {"expert": b}).wait_send()

        return carry

    def drain_factor():
        for i in range(each):
            to = target_of(z, i)

            @pl.when(to != col)
            def _(i=i, to=to):
                remote(fsend.at[i], frecv.at[0], f_s.at[i], f_r.at[0], {"expert": to}).wait_send()

    def step_chunks(t):
        return [ring_block(t, 0), ring_block(t, 1)] if t < half - 1 else [ring_block(t, 0)]

    def combine(total, ks):
        for k in ks:
            for i in range(each):
                src = target_of(k, i)

                @pl.when(src != col)
                def _(src=src):
                    remote(osend.at[0], oret.at[src], o_s.at[0], o_r.at[src], {"expert": src}).wait_recv()

            p = lax.rem(col // each + chips + chips - k, chips)
            back = oret[pl.ds(p * each, each)].reshape(each * unit, out.shape[1])
            total = total + jnp.dot(chi[p], back, preferred_element_type=F32)
            total = total + jnp.dot(clo[p], back, preferred_element_type=F32)
        return total

    total = jnp.zeros(out.shape, F32)
    pending = [(z * each + u, [own_hand(other, u, w) for w in range(2)]) for u in range(each)]
    for t in range(half):
        if t == half - 1:
            complete(pending)
            pending = []
            total = combine(total, [z])
            for early_step in range(half - 3):
                total = combine(total, step_chunks(early_step))
        fresh = []
        for u in range(each):
            for d in range(2):
                if not goes(t, d, u):
                    continue
                fresh.append(
                    (ring_block(t, d) * each + u, [hand(other, d, t, u, w, ring_block(t, d) * each + u) for w in range(2)])
                )
            for w in range(2):
                for d in range(2):
                    if not goes(t, d, u):
                        continue
                    b = ring_block(t, d) * each + u
                    spread(d, t, u, w, b).wait_recv()
                    if goes(t + 1, d, u):
                        start(spread(d, t + 1, u, w, b))
                    start(hand(c, d, t, u, w, b))
        if pending:
            complete(pending)
        if t == 0:
            lax.fori_loop(0, chips, drain, 0)
            lax.fori_loop(0, e, drain_rows, 0)
            drain_factor()
        if t == half - 1 and half > 2:
            total = combine(total, step_chunks(half - 3))
        pending = fresh
    complete(pending)

    for t in range(max(half - 2, 0), half):
        total = combine(total, step_chunks(t))
    out[...] = total.astype(BF16)

    for copy in sent:
        copy.wait_send()

    def drain_out(b, carry):
        target = lax.rem(b + shift, e)

        @pl.when(target != col)
        def _():
            remote(osend.at[b], oret.at[col], o_s.at[b], o_r.at[col], {"expert": target}).wait_send()

        return carry

    lax.fori_loop(0, e, drain_out, 0)


def on_device(
    n, e, queries, prompt_kv, gen_kv, gen_lengths, out_proj, residual, norm_gain,
    w_gate_up, w_down, routes, route_probs,
):
    prompts = queries.shape[0]
    rows = prompts * n
    features = residual.shape[2]
    out_features = w_down.shape[2]
    chips = n // 2
    half = chips // 2
    each = e // chips
    unit = -(-EXP_COL * CAP // TILE) * TILE
    heads = queries.shape[2] // HDIM
    topk = routes.shape[2]
    width = HERE * GROUPS * HDIM
    wide = HERE * HDIM
    tokens, gen = prompt_kv.shape[1], gen_kv.shape[2]
    quarter = w_gate_up.shape[2] // 8
    table = 128
    hbm = pl.BlockSpec(memory_space=pltpu.HBM)
    vmem = pl.BlockSpec(memory_space=pltpu.VMEM)
    dma = pltpu.SemaphoreType.DMA
    buf = pltpu.VMEM
    mixed, expert_out = pl.pallas_call(
        functools.partial(kernel, n, e),
        out_shape=(
            pltpu.VMEM((rows, features), BF16),
            pltpu.VMEM((rows, out_features), BF16),
        ),
        in_specs=[hbm] * 11,
        out_specs=(vmem, vmem),
        scratch_shapes=[
            buf((prompts, heads * HDIM), BF16),
            buf((prompts, heads, HDIM), F32),
            buf((prompts, heads, HDIM), BF16),
            buf((1, prompts), jnp.int32),
            buf((rows, features), BF16),
            buf((1, features), F32),
            buf((prompts, topk, n), jnp.int32),
            buf((prompts, topk, n), F32),
            buf((prompts, 2, tokens, 2 * wide), BF16),
            buf((prompts, gen, gen_kv.shape[3]), BF16),
            buf((prompts, 2, (HERE + 1) * GROUPS, HDIM), BF16),
            buf((n, HERE * GROUPS, HDIM), BF16),
            buf((n, (HERE + 1) * GROUPS, HDIM), BF16),
            buf((n, tokens, 2 * wide), BF16),
            buf((2, width, features), BF16),
            buf(w_gate_up.shape, BF16),
            buf(w_down.shape, BF16),
            buf((HERE, n * GROUPS, HDIM), F32),
            buf((HERE, n * GROUPS, HDIM), F32),
            buf((HERE, n * GROUPS, HDIM), F32),
            buf((HERE, n * GROUPS, HDIM), BF16),
            buf((2, rows, width), BF16),
            buf((8, rows), F32),
            buf((n, 8, rows), F32),
            buf((rows, table), BF16),
            buf((e, unit, rows), BF16),
            buf((chips, rows, each * unit), BF16),
            buf((chips, rows, each * unit), BF16),
            buf((rows, features), BF16),
            buf((e, unit, features), BF16),
            buf((e, unit, features), BF16),
            buf((2, e, 2, unit, quarter), BF16),
            buf((2, e, 2, unit, quarter), BF16),
            buf((2, e, 2, unit, quarter), BF16),
            buf((2, chips - 1, each, 2, unit, quarter), BF16),
            buf((2, e, 2, unit, quarter), BF16),
            buf((e, unit, out_features), BF16),
            buf((e, unit, out_features), BF16),
            buf((each, unit, HDIM), F32),
            buf((each, unit, HDIM), F32),
            dma((17,)),
            dma((3, n)),
            dma((3, n)),
            dma((2, half, PIECES)),
            dma((2, half, PIECES)),
            dma((2, half, PIECES)),
            dma((2, half, PIECES)),
            dma((2, PIECES)),
            dma((n,)),
            dma((n,)),
            dma((e,)),
            dma((e,)),
            dma((2, chips)),
            dma((2, chips)),
            dma((2, chips - 1, each, 2)),
            dma((2, chips - 1, each, 2)),
            dma((2, half, each, 2)),
            dma((2, half, each, 2)),
            dma((2, half, each, 2)),
            dma((2, half, each, 2)),
            dma((2, each, 2)),
            dma((e,)),
            dma((e,)),
            dma((each,)),
            dma((each,)),
        ],
        compiler_params=pltpu.CompilerParams(
            collective_id=0, has_side_effects=True, vmem_limit_bytes=56 << 20
        ),
        name="decode_step",
    )(
        queries.reshape(prompts, heads * HDIM),
        gen_lengths.T,
        prompt_kv,
        gen_kv.reshape(prompts, gen, gen_kv.shape[3]),
        out_proj.reshape(2, width, features),
        residual.reshape(rows, features),
        norm_gain.reshape(1, features),
        jnp.swapaxes(routes, 1, 2),
        jnp.swapaxes(route_probs, 1, 2),
        w_gate_up,
        w_down,
    )
    shape = (prompts, n, features)
    return (mixed.reshape(shape), expert_out.reshape(shape))


def solution(mesh):
    placed = (
        P("expert", "sample", None),
        P("expert", "sample", None),
        P("expert", "sample", None, None),
        P("expert", "sample"),
        P(None, "sample"),
        P("expert", None, "sample"),
        P("sample"),
        P("expert", "sample", None),
        P("expert", None, "sample"),
        P("expert", None, None),
        P("expert", None, None),
    )
    return jax.shard_map(
        functools.partial(on_device, mesh.shape["sample"], mesh.shape["expert"]),
        mesh=mesh,
        in_specs=placed,
        out_specs=(P("expert", None, "sample"), P("expert", None, "sample")),
        check_vma=False,
    )
```
